512 devices in a mesh: seq: 128 (over z_lo, x, y), head: 4 (over z_hi, core).
Axes of the slice: x: 4, y: 8, z: 8 (z_hi: 2, z_lo: 4; z = z_hi * 4 + z_lo), core: 2. Of those that a mesh axis runs over, the one named last changes fastest.
Arguments:
- queries: bfloat16 [16384, 2048], P('seq', 'head'), may hold values from -150 to 150
- keys: bfloat16 [16384, 1024], P('seq', 'head'), may hold values from -5 to 5
- values: bfloat16 [16384, 1024], P('seq', 'head'), may hold values from -5 to 5
- prefix_resid: bfloat16 [16384, 5376], P('seq', 'head'), may hold values from -6 to 6
- opt_queries: bfloat16 [128, 64, 2048], P('seq', None, 'head'), may hold values from -150 to 150
- opt_keys: bfloat16 [128, 64, 1024], P('seq', None, 'head'), may hold values from -5 to 5
- opt_values: bfloat16 [128, 64, 1024], P('seq', None, 'head'), may hold values from -5 to 5
- opt_resid: bfloat16 [128, 64, 5376], P('seq', None, 'head'), may hold values from -6 to 6
- out_weight: bfloat16 [2048, 5376], P('seq', 'head'), may hold values from -0.5347495 to 0.5347495
- norm_gain: float32 [5376], P('head'), may hold values from 0.1 to 1.9
- option_bounds: int32 [128, 2], P('seq'), may hold values from 0 to 64, as said below
Outputs:
- prefix_out: bfloat16 [16384, 5376], P('seq', 'head')
- option_out: bfloat16 [128, 64, 5376], P('seq', None, 'head')
- option_summary: float32 [128, 5376], P('seq', 'head')
The draws below stay inside these ranges and needn't reach their ends.
Inputs may be any that keep to these rules, and one draw needn't show every extreme that they name: `option_bounds`: column 0 is an option's first answer position and column 1 its length, with 0 <= start < length; some option has length 64.
All inputs are finite; a program needn't handle non-finite values.
Results may differ from the reference program's by a relative error of at most 0.009.
Values may be sent and summed in bfloat16 or wider, within the bound.
A program may use at most 64 MiB of HBM per device.

```python
import jax
import jax.numpy as jnp
from jax import lax

D = 5376
HQ = 16
KVH = 8
HD = 128
WINDOW = 1024
TOK_DEV = 128
OPT_LEN = 64
TOKENS = 16384
OPTIONS = 128
N_HEAD = 4


def drawn_keys(key):
    base_key = jax.random.fold_in(key, 101)
    first_key = jax.random.fold_in(base_key, 0)
    keys_all = jnp.clip(jax.random.normal(first_key, (TOKENS, KVH * HD), jnp.float32), -5.0, 5.0)
    return keys_all


def draw_keys(key, part):
    return drawn_keys(key).astype(jnp.bfloat16)


def draw_queries(key, part):
    result = jnp.clip(jax.random.normal(jax.random.fold_in(key, 202), (TOKENS, HQ * HD), jnp.float32), -5.0, 5.0)
    return result.astype(jnp.bfloat16)


def draw_opt_queries(key, part):
    result = jnp.clip(jax.random.normal(jax.random.fold_in(key, 303), (OPTIONS, OPT_LEN, HQ * HD), jnp.float32), -5.0, 5.0)
    return result.astype(jnp.bfloat16)


def draw_out_weight(key, part):
    first_key, second_key = jax.random.split(jax.random.fold_in(key, 404), 2)
    base = jnp.clip(jax.random.normal(first_key, (HQ * HD, D), jnp.float32), -4.0, 4.0)
    column_pos = jnp.arange(D, dtype=jnp.float32) / (D - 1)
    column_scale = 3.0 ** column_pos * jnp.exp(jax.random.uniform(second_key, (D,), jnp.float32, -0.7, 0.7))
    return (base * column_scale[None, :] / jnp.sqrt(jnp.float32(HQ * HD))).astype(jnp.bfloat16)


def draw_option_bounds(key, part):
    first_key, second_key, third_key = jax.random.split(jax.random.fold_in(key, 505), 3)
    length = jax.random.randint(first_key, (OPTIONS,), 1, OPT_LEN + 1)
    longest = jax.random.randint(second_key, (), 0, OPTIONS)
    length = length.at[longest].set(OPT_LEN)
    start_pos = jax.random.randint(third_key, (OPTIONS,), 0, OPT_LEN) % length
    return jnp.stack([start_pos, length], axis=1).astype(jnp.int32)


def steps_of(key, shape, cuts, smallest, largest):
    gain = 1.0
    for position, shards_of in cuts:
        draws = jax.random.uniform(jax.random.fold_in(jax.random.fold_in(key, 6), position), (shards_of,), jnp.float32, smallest / len(cuts), largest / len(cuts))
        gain = gain * jnp.repeat(jnp.exp(draws), shape[position] // shards_of).reshape((-1,) + (1,) * (len(shape) - 1 - position))
    return gain


def normal_values(rng, shape, scale, reach, cuts=(), kind=jnp.bfloat16):
    values = scale * jax.random.normal(rng, shape, jnp.float32)
    if cuts:
        values = values * steps_of(rng, shape, cuts, -0.22, 0.18)
    return jnp.clip(values, -reach, reach).astype(kind)


def setup_inputs(seed: int = 0) -> dict:
    arg_keys = jax.random.split(jax.random.key(seed), 12)
    return {
        "queries": draw_queries(jax.random.fold_in(arg_keys[11], 71), 0),
        "keys": draw_keys(jax.random.fold_in(arg_keys[11], 71), 0),
        "values": normal_values(arg_keys[2], (TOKENS, KVH * HD), 1.0, 5.0, ((0, 128), (1, 4))),
        "prefix_resid": normal_values(arg_keys[3], (TOKENS, D), 1.0, 6.0, ((0, 128), (1, 4))),
        "opt_queries": draw_opt_queries(jax.random.fold_in(arg_keys[11], 71), 0),
        "opt_keys": normal_values(arg_keys[5], (OPTIONS, OPT_LEN, KVH * HD), 1.0, 5.0, ((0, 128), (2, 4))),
        "opt_values": normal_values(arg_keys[6], (OPTIONS, OPT_LEN, KVH * HD), 1.0, 5.0, ((0, 128), (2, 4))),
        "opt_resid": normal_values(arg_keys[7], (OPTIONS, OPT_LEN, D), 1.0, 6.0, ((0, 128), (2, 4))),
        "out_weight": draw_out_weight(jax.random.fold_in(arg_keys[11], 71), 0),
        "norm_gain": jnp.clip(1.0 + 0.18 * jax.random.normal(arg_keys[9], (D,), jnp.float32), 0.1, 1.9),
        "option_bounds": draw_option_bounds(jax.random.fold_in(arg_keys[11], 71), 0),
    }


score_scale = 168.0 ** (-0.5)
epsilon = 1e-06

def attend(query_rows, key_rows, value_rows, allowed):
    row_count = query_rows.shape[0]
    kv_heads = key_rows.shape[1] // HD
    groups = query_rows.shape[1] // key_rows.shape[1]
    query_view = query_rows.astype(jnp.float32).reshape(row_count, kv_heads, groups, HD)
    key_view = key_rows.astype(jnp.float32).reshape(-1, kv_heads, HD)
    scores = jnp.einsum('rkgd,lkd->kgrl', query_view, key_view) * score_scale
    scores = jnp.where(allowed[None, None], scores, -jnp.inf)
    row_max = lax.optimization_barrier(jnp.max(scores, axis=-1, keepdims=True))
    weights = jnp.exp(scores - row_max)
    weights = (weights / lax.optimization_barrier(jnp.sum(weights, axis=-1, keepdims=True))).astype(jnp.bfloat16)
    value_view = value_rows.astype(jnp.float32).reshape(-1, kv_heads, HD)
    attended = jnp.einsum('kgrl,lkd->rkgd', weights.astype(jnp.float32), value_view)
    return attended.reshape(row_count, -1).astype(jnp.bfloat16)

def project_norm(stacked, out_weight, norm_gain):
    head_cols = HQ * HD // N_HEAD
    projected = jnp.zeros((stacked.shape[0], D), jnp.float32)
    for group in range(N_HEAD):
        partial_value = jnp.dot(stacked[:, group * head_cols:(group + 1) * head_cols], out_weight[group * head_cols:(group + 1) * head_cols], preferred_element_type=jnp.float32)
        projected = projected + lax.optimization_barrier(partial_value.astype(jnp.bfloat16)).astype(jnp.float32)
    mean_square = lax.optimization_barrier(jnp.mean(projected * projected, axis=-1, keepdims=True))
    return projected * lax.rsqrt(mean_square + epsilon) * norm_gain.astype(jnp.float32)

def reference(queries, keys, values, prefix_resid, opt_queries, opt_keys, opt_values, opt_resid, out_weight, norm_gain, option_bounds):
    padded_keys = jnp.concatenate([jnp.zeros((WINDOW, keys.shape[1]), keys.dtype), keys], axis=0)
    padded_values = jnp.concatenate([jnp.zeros((WINDOW, values.shape[1]), values.dtype), values], axis=0)

    def prefix_block(block_index):
        first_row = block_index * TOK_DEV
        block_queries = lax.dynamic_slice_in_dim(queries, first_row, TOK_DEV, 0)
        block_keys = lax.dynamic_slice_in_dim(padded_keys, first_row, WINDOW + TOK_DEV, 0)
        block_values = lax.dynamic_slice_in_dim(padded_values, first_row, WINDOW + TOK_DEV, 0)
        query_pos = first_row + jnp.arange(TOK_DEV, dtype=jnp.int32)
        key_pos = first_row - WINDOW + jnp.arange(WINDOW + TOK_DEV, dtype=jnp.int32)
        allowed = (key_pos[None] <= query_pos[:, None]) & (key_pos[None] > query_pos[:, None] - WINDOW) & (key_pos[None] >= 0)
        return attend(block_queries, block_keys, block_values, allowed)
    prefix_attn = lax.map(prefix_block, jnp.arange(TOKENS // TOK_DEV, dtype=jnp.int32)).reshape(TOKENS, -1)
    last_keys = keys[TOKENS - WINDOW:]
    last_values = values[TOKENS - WINDOW:]
    positions = jnp.arange(WINDOW + OPT_LEN, dtype=jnp.int32)
    option_pos = jnp.arange(OPT_LEN, dtype=jnp.int32)
    option_allowed = jnp.where(positions[None] < WINDOW, positions[None] > option_pos[:, None], positions[None] - WINDOW <= option_pos[:, None])

    def option_block(inputs):
        option_queries, own_keys, own_values = inputs
        joined_keys = jnp.concatenate([last_keys, own_keys], axis=0)
        joined_values = jnp.concatenate([last_values, own_values], axis=0)
        return attend(option_queries, joined_keys, joined_values, option_allowed)
    option_attn = lax.map(option_block, (opt_queries, opt_keys, opt_values)).reshape(OPTIONS * OPT_LEN, -1)
    prefix_normed = project_norm(prefix_attn, out_weight, norm_gain)
    option_normed = project_norm(option_attn, out_weight, norm_gain)
    prefix_out = (prefix_resid.astype(jnp.float32) + prefix_normed).astype(jnp.bfloat16)
    option_full = opt_resid.astype(jnp.float32) + option_normed.reshape(OPTIONS, OPT_LEN, D)
    start_pos = option_bounds[:, 0]
    length = option_bounds[:, 1]
    inside = option_pos[None, :] < length[:, None]
    option_out = jnp.where(inside[:, :, None], option_full, 0.0).astype(jnp.bfloat16)
    chosen = inside & (option_pos[None, :] >= start_pos[:, None])
    option_summary = lax.optimization_barrier(jnp.sum(jnp.where(chosen[:, :, None], option_out.astype(jnp.float32), 0.0), axis=1)) / (length - start_pos).astype(jnp.float32)[:, None]
    return (prefix_out, option_out, option_summary)
```

```python
import jax
import jax.numpy as jnp
from jax import lax
from jax.experimental import pallas as pl
from jax.experimental.pallas import tpu as pltpu
from jax.sharding import PartitionSpec as P

D = 5376
HD = 128
WINDOW = 1024
TOK = 128
OPT = 64
COLS = 1344
NY = 8
ROWS = TOK + OPT
MESH = pl.DeviceIdType.MESH

score_scale = 168.0 ** (-0.5)
epsilon = 1e-06
exp2_scale = score_scale * 1.4426950408889634

WYP, WYM = 0, 4
UP, DOWN = 8, 16
TREE, LP, LM = 24, 25, 30
WZ, XL, XR, HL, HR = 34, 38, 42, 46, 50
HEADS, SQ = 54, 60
N_RECV = 64
N_SEND = 96


def softmax_dot(scores, value_rows):
    top = jnp.max(scores, axis=1, keepdims=True)
    weights = jnp.exp2((scores - top) * exp2_scale)
    total = jnp.sum(weights, axis=1, keepdims=True)
    out = jnp.dot(weights.astype(jnp.bfloat16), value_rows, preferred_element_type=jnp.float32)
    return out / total


def score_dot(query_rows, key_rows):
    return lax.dot_general(
        query_rows, key_rows, (((1,), (1,)), ((), ())), preferred_element_type=jnp.float32
    )


def kernel(
    q_in, k_in, v_in, res_in, oq_in, ok_in, ov_in, ores_in, w_in, gain_in, bounds,
    pout, oout, osum,
    q, oq, ok, ov, res, ores, gain, kv, lkv, wbuf, abuf, proj, ssq,
    local_sem, send_sem, recv_sem,
):
    seq = lax.axis_index("seq")
    head = lax.axis_index("head")
    z = lax.div(seq, 32)
    x = lax.rem(lax.div(seq, 8), 4)
    y = lax.rem(seq, 8)
    zhi = lax.div(head, 2)
    core = lax.rem(head, 2)
    group = z * 4 + x

    def at(zz, xx, yy):
        return ((zz * 4 + xx) * 8 + yy, head)

    up_y = at(z, x, lax.rem(y + 1, 8))
    down_y = at(z, x, lax.rem(y + 7, 8))
    up_x = at(z, lax.rem(x + 1, 4), y)
    down_x = at(z, lax.rem(x + 3, 4), y)
    up_z = at(lax.rem(z + 1, 4), x, y)
    down_z = at(lax.rem(z + 3, 4), x, y)
    next_line = (lax.rem(seq + 8, 128), head)
    prev_line = (lax.rem(seq + 120, 128), head)
    h_sib = zhi * 2 + 1 - core
    h_far = (1 - zhi) * 2 + core
    h_farsib = (1 - zhi) * 2 + 1 - core
    sib = (seq, h_sib)
    far = (seq, h_far)
    farsib = (seq, h_farsib)

    local = []

    def load(src, dst, pred=None):
        copy = pltpu.make_async_copy(src, dst, local_sem.at[len(local)])
        local.append(copy)
        if pred is None:
            copy.start()
        else:
            pl.when(pred)(lambda: copy.start())
        return copy

    def rows16(g, yy):
        return wbuf.at[pl.ds(pl.multiple_of(g * 128 + yy * 16, 16), 16), :]

    def rows128(g):
        return wbuf.at[pl.ds(pl.multiple_of(g * 128, 128), 128), :]

    def rows64(g, half):
        return wbuf.at[pl.ds(pl.multiple_of(g * 128 + half * 64, 64), 64), :]

    is_source = (z == 3) & (x == 3)
    first = [
        load(k_in, kv.at[8, :, pl.ds(0, 256)]),
        load(v_in, kv.at[8, :, pl.ds(256, 256)]),
        load(w_in, rows16(group, y)),
    ]
    source_loads = [
        load(k_in, lkv.at[y, :, pl.ds(0, 256)], is_source),
        load(v_in, lkv.at[y, :, pl.ds(256, 256)], is_source),
    ]
    later = [
        load(q_in, q), load(oq_in, oq), load(ok_in, ok), load(ov_in, ov),
        load(res_in, res), load(ores_in, ores), load(gain_in, gain),
    ]

    barrier = pltpu.get_barrier_semaphore()
    partners = [up_y, down_y, up_x, down_x, up_z, down_z, next_line, prev_line, sib, far, farsib]
    for partner in partners:
        pl.semaphore_signal(barrier, inc=1, device_id=partner, device_id_type=MESH)
    for copy in first:
        copy.wait()

    @pl.when(is_source)
    def _():
        for copy in source_loads:
            copy.wait()

    pl.semaphore_wait(barrier, len(partners))

    sent = []

    def send(src, dst, recv, device, pred=None):
        copy = pltpu.make_async_remote_copy(
            src_ref=src, dst_ref=dst, send_sem=send_sem.at[len(sent)],
            recv_sem=recv_sem.at[recv], device_id=device, device_id_type=MESH,
        )
        sent.append((copy, pred))
        if pred is None:
            copy.start()
        else:
            pl.when(pred)(lambda: copy.start())

    def arrived(ref, recv, pred=None):
        copy = pltpu.make_async_remote_copy(
            src_ref=ref, dst_ref=ref, send_sem=send_sem.at[0],
            recv_sem=recv_sem.at[recv], device_id=sib, device_id_type=MESH,
        )
        if pred is None:
            copy.wait_recv()
        else:
            pl.when(pred)(lambda: copy.wait_recv())

    def mod8(value):
        return lax.rem(value + 8, 8)

    def wy_up(k):
        piece = rows16(group, mod8(y - k))
        if k:
            arrived(piece, WYP + k - 1)
        if k < 4:
            send(piece, piece, WYP + k, up_y)

    def wy_down(k):
        piece = rows16(group, lax.rem(y + k, 8))
        if k:
            arrived(piece, WYM + k - 1)
        if k < 3:
            send(piece, piece, WYM + k, down_y)

    def kv_up(k):
        if k:
            arrived(kv.at[8 - k], UP + k, y >= k)
        if k < 7:
            send(kv.at[8 - k], kv.at[7 - k], UP + k + 1, up_y, (y >= k) & (y < 7))

    def kv_down(m):
        arrived(kv.at[m], DOWN + m, y <= 7 - m)
        if m < 7:
            send(kv.at[m], kv.at[m + 1], DOWN + m + 1, down_y, (y <= 7 - m) & (y > 0))

    depth = lax.select(x == 3, 0, lax.select(x == 1, 2, 1)) + 3 - z

    def tree_sends(pred):
        piece = lkv.at[y]
        send(piece, piece, TREE, up_x, pred & (z == 3) & ((x == 3) | (x == 0)))
        send(piece, piece, TREE, down_x, pred & (z == 3) & (x == 3))
        send(piece, piece, TREE, down_z, pred & (z > 0))

    def tree(k):
        here = depth == k
        if k:
            arrived(lkv.at[y], TREE, here)
        tree_sends(here)

    def l_up(k):
        piece = lkv.at[mod8(y - k)]
        if k:
            arrived(piece, LP + k)
        if k < 4:
            send(piece, piece, LP + k + 1, up_y)

    def l_down(k):
        piece = lkv.at[lax.rem(y + k, 8)]
        if k:
            arrived(piece, LM + k)
        if k < 3:
            send(piece, piece, LM + k + 1, down_y)

    zhalf = lax.div(z, 2)
    order = [
        z,
        z - 1 + 2 * (1 - lax.div(z + 3, 4)),
        2 + zhalf * (1 - 2 * lax.rem(z, 2)),
        3 * (1 - zhalf),
    ]

    def z_event(i):
        plane = order[i]
        piece = rows128(plane * 4 + x)
        if i:
            arrived(piece, WZ + plane)
        send(piece, piece, WZ + plane, up_z, (plane <= z) & (z < 3))
        send(piece, piece, WZ + plane, down_z, (plane >= z) & (z > 0))
        send(piece, piece, XL + i, up_x)
        send(piece, piece, XR + i, down_x)

    def x_full(i):
        left = order[i] * 4 + lax.rem(x + 3, 4)
        right = order[i] * 4 + lax.rem(x + 1, 4)
        arrived(rows128(left), XL + i)
        send(rows64(left, 0), rows64(left, 0), HL + i, up_x)
        arrived(rows128(right), XR + i)
        send(rows64(right, 1), rows64(right, 1), HR + i, down_x)

    def x_half(i):
        across = order[i] * 4 + lax.rem(x + 2, 4)
        arrived(rows64(across, 0), HL + i)
        arrived(rows64(across, 1), HR + i)

    def prefix_pair(i):
        keys = kv[:, :, i * HD:(i + 1) * HD].reshape(9 * TOK, HD)
        vals = kv[:, :, 256 + i * HD:256 + (i + 1) * HD].reshape(9 * TOK, HD)
        for half in range(2):
            c = (2 * i + half) * HD
            scores = score_dot(q[:, c:c + HD], keys)
            row = lax.broadcasted_iota(jnp.int32, scores.shape, 0)
            col = lax.broadcasted_iota(jnp.int32, scores.shape, 1)
            allowed = (col > row) & (col <= row + WINDOW) & (col >= (8 - seq) * TOK)
            scores = jnp.where(allowed, scores, -jnp.inf)
            abuf[head, 0:TOK, c:c + HD] = softmax_dot(scores, vals).astype(jnp.bfloat16)

    def option_pair(i):
        keys = lkv[:, :, i * HD:(i + 1) * HD].reshape(WINDOW, HD)
        vals = lkv[:, :, 256 + i * HD:256 + (i + 1) * HD].reshape(WINDOW, HD)
        own_keys = ok[:, i * HD:(i + 1) * HD]
        own_vals = ov[:, i * HD:(i + 1) * HD]
        for half in range(2):
            c = (2 * i + half) * HD
            query = oq[:, c:c + HD]
            shared = score_dot(query, keys)
            own = score_dot(query, own_keys)
            row = lax.broadcasted_iota(jnp.int32, shared.shape, 0)
            col = lax.broadcasted_iota(jnp.int32, shared.shape, 1)
            shared = jnp.where(col > row, shared, -jnp.inf)
            row = lax.broadcasted_iota(jnp.int32, own.shape, 0)
            col = lax.broadcasted_iota(jnp.int32, own.shape, 1)
            own = jnp.where(col <= row, own, -jnp.inf)
            top = jnp.maximum(
                jnp.max(shared, axis=1, keepdims=True), jnp.max(own, axis=1, keepdims=True)
            )
            ws = jnp.exp2((shared - top) * exp2_scale)
            wo = jnp.exp2((own - top) * exp2_scale)
            total = jnp.sum(ws, axis=1, keepdims=True) + jnp.sum(wo, axis=1, keepdims=True)
            out = jnp.dot(ws.astype(jnp.bfloat16), vals, preferred_element_type=jnp.float32)
            out = out + jnp.dot(
                wo.astype(jnp.bfloat16), own_vals, preferred_element_type=jnp.float32
            )
            abuf[head, TOK:ROWS, c:c + HD] = (out / total).astype(jnp.bfloat16)

    def exchange_send(part):
        rows = pl.ds(0, TOK) if part == 0 else pl.ds(TOK, OPT)
        piece = abuf.at[head, rows, :]
        send(piece, piece, HEADS + 3 * part, far_first[0])
        send(piece, piece, HEADS + 3 * part + 1, far_first[1])

    far_first = (far, sib)

    def exchange_forward(part):
        rows = pl.ds(0, TOK) if part == 0 else pl.ds(TOK, OPT)
        piece = abuf.at[h_far, rows, :]
        arrived(piece, HEADS + 3 * part)
        send(piece, piece, HEADS + 3 * part + 2, sib)

    def exchange_rest(part):
        rows = pl.ds(0, TOK) if part == 0 else pl.ds(TOK, OPT)
        arrived(abuf.at[h_sib, rows, :], HEADS + 3 * part + 1)
        arrived(abuf.at[h_farsib, rows, :], HEADS + 3 * part + 2)

    def project(i):
        plane = order[i]
        part = jnp.dot(
            abuf[plane], wbuf[pl.ds(pl.multiple_of(plane * 512, 512), 512), :],
            preferred_element_type=jnp.float32,
        )
        if i == 0:
            proj[...] = part
        else:
            proj[...] += part

    wy_up(0)
    wy_down(0)
    kv_up(0)
    send(kv.at[8], kv.at[0], DOWN, next_line)
    tree(0)
    for k in range(1, 8):
        kv_down(k - 1)
        kv_up(k)
        if k <= 4:
            wy_up(k)
        if k <= 3:
            wy_down(k)
        if k == 4:
            z_event(0)
        if k <= 5:
            tree(k)
        if k == 6:
            z_event(1)
        if k == 7:
            x_full(0)
    kv_down(7)
    l_up(0)
    l_down(0)
    for copy in later[:4]:
        copy.wait()
    prefix_pair(0)
    l_up(1)
    l_down(1)
    z_event(2)
    prefix_pair(1)
    exchange_send(0)
    l_up(2)
    l_down(2)
    x_full(1)
    l_up(3)
    l_down(3)
    exchange_forward(0)
    l_up(4)
    option_pair(0)
    option_pair(1)
    exchange_send(1)
    z_event(3)
    x_full(2)
    exchange_rest(0)
    exchange_forward(1)
    exchange_rest(1)
    x_half(0)
    project(0)
    x_full(3)
    for i in range(1, 4):
        x_half(i)
        project(i)

    square = jnp.sum(proj[...] * proj[...], axis=1, keepdims=True)
    diag = (
        lax.broadcasted_iota(jnp.int32, (128, 128), 0)
        == lax.broadcasted_iota(jnp.int32, (128, 128), 1)
    )
    row0 = jnp.sum(jnp.where(diag, square[0:128], 0.0), axis=0, keepdims=True)
    row1 = jnp.sum(jnp.where(diag[0:64], square[128:192], 0.0), axis=0, keepdims=True)
    ssq[head] = jnp.concatenate([row0, row1, jnp.zeros((6, 128), jnp.float32)], axis=0)
    mine = ssq.at[head]
    send(mine, mine, SQ, far)
    send(mine, mine, SQ + 1, farsib)
    send(mine, mine, SQ + 2, sib)
    for copy in later[4:]:
        copy.wait()
    arrived(ssq.at[h_sib], SQ + 2)
    arrived(ssq.at[h_far], SQ)
    arrived(ssq.at[h_farsib], SQ + 1)
    total = ssq[0] + ssq[1] + ssq[2] + ssq[3]
    col0 = jnp.sum(jnp.where(diag, total[0:1], 0.0), axis=1, keepdims=True)
    col1 = jnp.sum(jnp.where(diag[0:64], total[1:2], 0.0), axis=1, keepdims=True)
    inv0 = lax.rsqrt(col0 / D + epsilon)
    inv1 = lax.rsqrt(col1 / D + epsilon)
    pout[...] = (
        res[...].astype(jnp.float32) + proj[0:TOK, :] * inv0 * gain[...]
    ).astype(jnp.bfloat16)
    full = ores[...].astype(jnp.float32) + proj[TOK:ROWS, :] * inv1 * gain[...]
    start = bounds[0, 0]
    length = bounds[0, 1]
    pos = lax.broadcasted_iota(jnp.int32, (OPT, COLS), 0)
    inside = pos < length
    out = jnp.where(inside, full, 0.0).astype(jnp.bfloat16)
    oout[...] = out
    chosen = inside & (pos >= start)
    picked = jnp.where(chosen, out.astype(jnp.float32), 0.0)
    count = jnp.broadcast_to((length - start).astype(jnp.float32), (1, COLS))
    osum[...] = jnp.sum(picked, axis=0, keepdims=True) / count

    for copy, pred in sent:
        if pred is None:
            copy.wait_send()
        else:
            pl.when(pred)(lambda copy=copy: copy.wait_send())


def fused(*args):
    bf, f32 = jnp.bfloat16, jnp.float32
    anywhere = pl.BlockSpec(memory_space=pl.ANY)
    vmem = pl.BlockSpec(memory_space=pltpu.VMEM)
    return pl.pallas_call(
        kernel,
        out_shape=(
            jax.ShapeDtypeStruct((TOK, COLS), bf),
            jax.ShapeDtypeStruct((OPT, COLS), bf),
            jax.ShapeDtypeStruct((1, COLS), f32),
        ),
        in_specs=[anywhere] * 10 + [pl.BlockSpec(memory_space=pltpu.SMEM)],
        out_specs=(vmem, vmem, vmem),
        scratch_shapes=[
            pltpu.VMEM((TOK, 512), bf),
            pltpu.VMEM((OPT, 512), bf),
            pltpu.VMEM((OPT, 256), bf),
            pltpu.VMEM((OPT, 256), bf),
            pltpu.VMEM((TOK, COLS), bf),
            pltpu.VMEM((OPT, COLS), bf),
            pltpu.VMEM((1, COLS), f32),
            pltpu.VMEM((9, TOK, 512), bf),
            pltpu.VMEM((8, TOK, 512), bf),
            pltpu.VMEM((2048, COLS), bf),
            pltpu.VMEM((4, ROWS, 512), bf),
            pltpu.VMEM((ROWS, COLS), f32),
            pltpu.VMEM((4, 8, 128), f32),
            pltpu.SemaphoreType.DMA((16,)),
            pltpu.SemaphoreType.DMA((N_SEND,)),
            pltpu.SemaphoreType.DMA((N_RECV,)),
        ],
        compiler_params=pltpu.CompilerParams(
            collective_id=0, has_side_effects=True, vmem_limit_bytes=48 * 1024 * 1024
        ),
    )(*args)


def body(
    queries, keys, values, prefix_resid, opt_queries, opt_keys, opt_values, opt_resid,
    out_weight, norm_gain, option_bounds,
):
    prefix_out, option_out, option_summary = fused(
        queries, keys, values, prefix_resid, opt_queries[0], opt_keys[0], opt_values[0],
        opt_resid[0], out_weight, norm_gain[None, :], option_bounds,
    )
    return prefix_out, option_out[None], option_summary[None, 0]


def solution(mesh):
    return jax.shard_map(
        body,
        mesh=mesh,
        in_specs=(
            P("seq", "head"),
            P("seq", "head"),
            P("seq", "head"),
            P("seq", "head"),
            P("seq", None, "head"),
            P("seq", None, "head"),
            P("seq", None, "head"),
            P("seq", None, "head"),
            P("seq", "head"),
            P("head"),
            P("seq", None),
        ),
        out_specs=(P("seq", "head"), P("seq", None, "head"), P("seq", "head")),
        check_vma=False,
    )
```

```python
import jax
import jax.numpy as jnp
from jax import lax
from jax.experimental import pallas as pl
from jax.experimental.pallas import tpu as pltpu
from jax.sharding import PartitionSpec as P

D = 5376
HD = 128
WINDOW = 1024
TOK = 128
OPT = 64
COLS = 1344
NY = 8
ROWS = TOK + OPT
MESH = pl.DeviceIdType.MESH

score_scale = 168.0 ** (-0.5)
epsilon = 1e-06
exp2_scale = score_scale * 1.4426950408889634

N_RECV = 128
N_SEND = 224


def softmax_dot(scores, value_rows):
    top = jnp.max(scores, axis=1, keepdims=True)
    weights = jnp.exp2((scores - top) * exp2_scale)
    total = jnp.sum(weights, axis=1, keepdims=True)
    out = jnp.dot(weights.astype(jnp.bfloat16), value_rows, preferred_element_type=jnp.float32)
    return out / total


def score_dot(query_rows, key_rows):
    return lax.dot_general(
        query_rows, key_rows, (((1,), (1,)), ((), ())), preferred_element_type=jnp.float32
    )


def kernel(
    q_in, k_in, v_in, res_in, oq_in, ok_in, ov_in, ores_in, w_in, gain_in, bounds,
    pout, oout, osum,
    q, oq, ok, ov, rest, res, ores, gain, kv, lkv, wbuf, abuf, relay, proj, ssq,
    local_sem, send_sem, recv_sem,
):
    seq = lax.axis_index("seq")
    head = lax.axis_index("head")
    z = lax.div(seq, 32)
    x = lax.rem(lax.div(seq, 8), 4)
    y = lax.rem(seq, 8)
    zhi = lax.div(head, 2)
    core = lax.rem(head, 2)
    group = z * 4 + x

    def at(zz, xx, yy):
        return ((zz * 4 + xx) * 8 + yy, head)

    up_y = at(z, x, lax.rem(y + 1, 8))
    down_y = at(z, x, lax.rem(y + 7, 8))
    up_y2 = at(z, x, lax.rem(y + 2, 8))
    down_y2 = at(z, x, lax.rem(y + 6, 8))
    next_half = (lax.rem(seq + 4, 128), head)
    prev_half = (lax.rem(seq + 124, 128), head)
    up_x = at(z, lax.rem(x + 1, 4), y)
    down_x = at(z, lax.rem(x + 3, 4), y)
    up_z = at(lax.rem(z + 1, 4), x, y)
    down_z = at(lax.rem(z + 3, 4), x, y)
    next_line = (lax.rem(seq + 8, 128), head)
    prev_line = (lax.rem(seq + 120, 128), head)
    h_sib = zhi * 2 + 1 - core
    h_far = (1 - zhi) * 2 + core
    h_farsib = (1 - zhi) * 2 + 1 - core
    sib = (seq, h_sib)
    far = (seq, h_far)
    farsib = (seq, h_farsib)
    z_mid = lax.rem(z + 2, 4)
    seq_mid = (z_mid * 4 + x) * 8 + y
    zhi_up = lax.rem(zhi + lax.div(z + 2, 4), 2)
    h_up = zhi_up * 2 + core
    h_down = (1 - zhi_up) * 2 + core
    mid_up = (seq_mid, h_up)
    mid_down = (seq_mid, h_down)

    local = []

    def load(src, dst, pred=None):
        copy = pltpu.make_async_copy(src, dst, local_sem.at[len(local)])
        local.append(copy)
        if pred is None:
            copy.start()
        else:
            pl.when(pred)(lambda: copy.start())
        return copy

    def rows16(g, yy):
        return wbuf.at[pl.ds(pl.multiple_of(g * 128 + yy * 16, 16), 16), :]

    def rows128(g):
        return wbuf.at[pl.ds(pl.multiple_of(g * 128, 128), 128), :]

    def rows64(g, half):
        return wbuf.at[pl.ds(pl.multiple_of(g * 128 + half * 64, 64), 64), :]

    is_source = (z == 3) & (x == 3)
    first = [
        load(w_in, rows16(group, y)),
        load(k_in, kv.at[0, 8]),
        load(v_in, kv.at[1, 8]),
    ]
    source_loads = [
        load(k_in, lkv.at[0, y], is_source),
        load(v_in, lkv.at[1, y], is_source),
    ]
    later = [
        load(res_in, rest),
        load(q_in, q), load(oq_in, oq), load(ok_in, ok), load(ov_in, ov),
        load(ores_in, ores), load(gain_in, gain),
    ]

    barrier = pltpu.get_barrier_semaphore()
    partners = [
        up_y, down_y, up_x, down_x, up_z, down_z, next_line, prev_line,
        sib, far, farsib, mid_up, mid_down, at(z_mid, x, y),
        up_y2, down_y2, next_half, prev_half,
    ]
    for partner in partners:
        pl.semaphore_signal(barrier, inc=1, device_id=partner, device_id_type=MESH)
    for copy in first:
        copy.wait()

    @pl.when(is_source)
    def _():
        for copy in source_loads:
            copy.wait()

    pl.semaphore_wait(barrier, len(partners))

    sent = []
    n_sent = [0]
    received = {}

    def recv_id(name, count=1):
        if name not in received:
            received[name] = recv_id.next
            recv_id.next += count
            assert recv_id.next <= N_RECV
        return received[name]

    recv_id.next = 0

    def remote(src, dst, recv, device):
        n_sent[0] += 1
        assert n_sent[0] <= N_SEND
        return pltpu.make_async_remote_copy(
            src_ref=src, dst_ref=dst, send_sem=send_sem.at[n_sent[0] - 1],
            recv_sem=recv_sem.at[recv], device_id=device, device_id_type=MESH,
        )

    def send(src, dst, recv, device, pred=None):
        copy = remote(src, dst, recv, device)
        sent.append((copy, pred))
        if pred is None:
            copy.start()
        else:
            pl.when(pred)(lambda: copy.start())

    def arrived(ref, recv, pred=None):
        copy = pltpu.make_async_remote_copy(
            src_ref=ref, dst_ref=ref, send_sem=send_sem.at[0],
            recv_sem=recv_sem.at[recv], device_id=sib, device_id_type=MESH,
        )
        if pred is None:
            copy.wait_recv()
        else:
            pl.when(pred)(lambda: copy.wait_recv())

    def drain():
        for copy, pred in sent:
            if pred is None:
                copy.wait_send()
            else:
                pl.when(pred)(lambda copy=copy: copy.wait_send())
        sent.clear()

    def mod8(value):
        return lax.rem(value + 8, 8)

    zhalf = lax.div(z, 2)
    order = [
        z,
        z - 1 + 2 * (1 - lax.div(z + 3, 4)),
        2 + zhalf * (1 - 2 * lax.rem(z, 2)),
        3 * (1 - zhalf),
    ]
    wz = recv_id("wz", 4)
    xl = [recv_id(("xl", i)) for i in range(4)]
    xr = [recv_id(("xr", i)) for i in range(4)]
    hl = [recv_id(("hl", i)) for i in range(4)]
    hr = [recv_id(("hr", i)) for i in range(4)]

    def spread(piece):
        send(piece, piece, xl[0], up_x)
        send(piece, piece, xr[0], down_x)
        send(piece, piece, wz + z, up_z, z < 3)
        send(piece, piece, wz + z, down_z, z > 0)

    def wy_piece(d):
        return rows16(group, mod8(y - d))

    def wy_id(d):
        return recv_id(("wy", d))

    def wy_start():
        piece = wy_piece(0)
        send(piece, piece, wy_id(2), up_y2)
        send(piece, piece, wy_id(-2), down_y2)
        send(piece, piece, wy_id(1), up_y)
        send(piece, piece, wy_id(-1), down_y)
        spread(piece)

    def wy_take(d):
        piece = wy_piece(d)
        arrived(piece, wy_id(d))
        if d == 2:
            send(piece, piece, wy_id(3), up_y)
            send(piece, piece, wy_id(4), up_y2)
        if d == -2:
            send(piece, piece, wy_id(-3), down_y)
        spread(piece)

    inner = (z == 1) | (z == 2)

    def x_send(i):
        piece = rows128(order[i] * 4 + x)
        send(piece, piece, xl[i], up_x)
        send(piece, piece, xr[i], down_x)

    def z_take(i, pred=None):
        arrived(rows128(order[i] * 4 + x), wz + order[i], pred)

    def z_near():
        z_take(1)
        piece = rows128(order[1] * 4 + x)
        send(piece, piece, wz + order[1], up_z, (order[1] < z) & inner)
        x_send(1)
        z_take(2, inner)
        piece = rows128(order[2] * 4 + x)
        send(piece, piece, wz + order[2], down_z, (order[2] > z) & inner)

    def z_mid_event():
        z_take(2, (z == 0) | (z == 3))
        z_take(3, inner)
        piece = rows128(order[3] * 4 + x)
        send(piece, piece, wz + order[3], down_z, z == 1)
        send(piece, piece, wz + order[3], up_z, z == 2)
        x_send(2)

    def z_last():
        z_take(3, (z == 0) | (z == 3))
        x_send(3)

    def x_full(i):
        left = order[i] * 4 + lax.rem(x + 3, 4)
        right = order[i] * 4 + lax.rem(x + 1, 4)
        arrived(rows128(left), xl[i])
        send(rows64(left, 0), rows64(left, 0), hl[i], up_x)
        arrived(rows128(right), xr[i])
        send(rows64(right, 1), rows64(right, 1), hr[i], down_x)

    def x_half(i):
        across = order[i] * 4 + lax.rem(x + 2, 4)
        arrived(rows64(across, 0), hl[i])
        arrived(rows64(across, 1), hr[i])

    def kv_send(p, slot, to_slot, device, pred=None):
        send(kv.at[p, slot], kv.at[p, to_slot], recv_id(("kv", to_slot, p)), device, pred)

    def kv_wait(p, slot, pred=None):
        arrived(kv.at[p, slot], recv_id(("kv", slot, p)), pred)

    def kv_own(p):
        kv_send(p, 8, 7, up_y, y < 7)
        kv_send(p, 8, 4, next_half)
        kv_send(p, 8, 0, next_line)

    def kv_near(r, p):
        if r <= 3:
            m = r - 1
            kv_wait(p, m, y <= 7 - m)
            kv_send(p, m, m + 1, down_y, (y <= 7 - m) & (y > 0))
            kv_wait(p, 8 - r, y >= r)
            if r < 3:
                kv_send(p, 8 - r, 7 - r, up_y, (y >= r) & (y < 7))
        else:
            kv_wait(p, 3, y <= 4)

    def kv_far(r, p):
        if r == 1:
            kv_wait(p, 4)
            kv_send(p, 4, 3, up_y, (y >= 4) & (y < 7))
            kv_send(p, 4, 5, down_y, (y < 4) & (y > 0))
            return
        k = 3 + r
        kv_wait(p, 8 - k, y >= k)
        kv_wait(p, k, y <= 7 - k)
        if k < 7:
            kv_send(p, 8 - k, 7 - k, up_y, (y >= k) & (y < 7))
            kv_send(p, k, k + 1, down_y, (y <= 7 - k) & (y > 0))

    depth = lax.select(x == 3, 0, lax.select(x == 1, 2, 1)) + 3 - z
    tree_up = (z == 3) & ((x == 3) | (x == 0))
    tree_down = (z == 3) & (x == 3)
    tree_copies = []
    for p in range(2):
        piece = lkv.at[p, y]
        tree_id = recv_id(("tree", p))
        for device, pred in ((up_x, tree_up), (down_x, tree_down), (down_z, z > 0)):
            tree_copies.append((remote(piece, piece, tree_id, device), pred))
    sent.extend(tree_copies)

    def tree(k, p):
        here = depth == k
        if k:
            arrived(lkv.at[p, y], recv_id(("tree", p)), here)
        for copy, pred in tree_copies[3 * p:3 * p + 3]:
            pl.when(here & pred)(lambda copy=copy: copy.start())

    def l_up(k, p):
        last = 4 - p
        if k > last:
            return
        piece = lkv.at[p, mod8(y - k)]
        if k:
            arrived(piece, recv_id(("lp", k, p)))
        if k < last:
            send(piece, piece, recv_id(("lp", k + 1, p)), up_y)

    def l_down(k, p):
        last = 3 + p
        if k > last:
            return
        piece = lkv.at[p, lax.rem(y + k, 8)]
        if k:
            arrived(piece, recv_id(("lm", k, p)))
        if k < last:
            send(piece, piece, recv_id(("lm", k + 1, p)), down_y)

    def l_step(k):
        for p in range(2):
            l_up(k, p)
            l_down(k, p)

    def prefix_pair(i):
        keys = kv[0, :, :, i * HD:(i + 1) * HD].reshape(9 * TOK, HD)
        vals = kv[1, :, :, i * HD:(i + 1) * HD].reshape(9 * TOK, HD)
        for half in range(2):
            c = (2 * i + half) * HD
            scores = score_dot(q[:, c:c + HD], keys)
            row = lax.broadcasted_iota(jnp.int32, scores.shape, 0)
            col = lax.broadcasted_iota(jnp.int32, scores.shape, 1)
            allowed = (col > row) & (col <= row + WINDOW) & (col >= (8 - seq) * TOK)
            scores = jnp.where(allowed, scores, -jnp.inf)
            abuf[head, i, 0:TOK, half * HD:(half + 1) * HD] = softmax_dot(
                scores, vals
            ).astype(jnp.bfloat16)

    def option_pair(i):
        keys = lkv[0, :, :, i * HD:(i + 1) * HD].reshape(WINDOW, HD)
        vals = lkv[1, :, :, i * HD:(i + 1) * HD].reshape(WINDOW, HD)
        own_keys = ok[:, i * HD:(i + 1) * HD]
        own_vals = ov[:, i * HD:(i + 1) * HD]
        for half in range(2):
            c = (2 * i + half) * HD
            query = oq[:, c:c + HD]
            shared = score_dot(query, keys)
            own = score_dot(query, own_keys)
            row = lax.broadcasted_iota(jnp.int32, shared.shape, 0)
            col = lax.broadcasted_iota(jnp.int32, shared.shape, 1)
            shared = jnp.where(col > row, shared, -jnp.inf)
            row = lax.broadcasted_iota(jnp.int32, own.shape, 0)
            col = lax.broadcasted_iota(jnp.int32, own.shape, 1)
            own = jnp.where(col <= row, own, -jnp.inf)
            top = jnp.maximum(
                jnp.max(shared, axis=1, keepdims=True), jnp.max(own, axis=1, keepdims=True)
            )
            ws = jnp.exp2((shared - top) * exp2_scale)
            wo = jnp.exp2((own - top) * exp2_scale)
            total = jnp.sum(ws, axis=1, keepdims=True) + jnp.sum(wo, axis=1, keepdims=True)
            out = jnp.dot(ws.astype(jnp.bfloat16), vals, preferred_element_type=jnp.float32)
            out = out + jnp.dot(
                wo.astype(jnp.bfloat16), own_vals, preferred_element_type=jnp.float32
            )
            abuf[head, i, TOK:ROWS, half * HD:(half + 1) * HD] = (out / total).astype(
                jnp.bfloat16
            )

    def part_rows(part):
        return pl.ds(0, TOK) if part == 0 else pl.ds(TOK, OPT)

    def exchange_send(part, i):
        rows = part_rows(part)
        piece = abuf.at[head, i, rows, :]
        send(piece, relay.at[i, rows, :], recv_id(("mid", part, i)), (mid_up, mid_down)[i])
        send(piece, piece, recv_id(("sib", part, i)), sib)

    def exchange_relay(part, i):
        rows = part_rows(part)
        piece = relay.at[i, rows, :]
        arrived(piece, recv_id(("mid", part, i)))
        origin = (h_down, h_up)[i]
        send(
            piece, abuf.at[origin, i, rows, :], recv_id(("far", part, i)),
            (mid_up, mid_down)[i],
        )

    def exchange_forward(part, i):
        piece = abuf.at[h_far, i, part_rows(part), :]
        arrived(piece, recv_id(("far", part, i)))
        send(piece, piece, recv_id(("farsib", part, i)), sib)

    def exchange_rest(part, i):
        arrived(abuf.at[h_sib, i, part_rows(part), :], recv_id(("sib", part, i)))
        arrived(abuf.at[h_farsib, i, part_rows(part), :], recv_id(("farsib", part, i)))

    def project(i):
        plane = order[i]
        part = None
        for pair in range(2):
            rows = pl.ds(pl.multiple_of(plane * 512 + pair * 256, 256), 256)
            new = jnp.dot(
                abuf[plane, pair], wbuf[rows, :], preferred_element_type=jnp.float32
            )
            part = new if part is None else part + new
        if i == 0:
            proj[...] = part
        else:
            proj[...] += part

    wy_start()
    tree(0, 0)
    tree(0, 1)
    wy_take(2)
    wy_take(-2)
    kv_own(0)
    kv_own(1)
    wy_take(1)
    wy_take(-1)
    tree(1, 0)
    tree(1, 1)
    wy_take(3)
    wy_take(-3)
    wy_take(4)
    kv_near(1, 0)
    kv_near(1, 1)
    z_near()
    x_full(0)
    kv_far(1, 0)
    kv_far(1, 1)
    tree(2, 0)
    tree(2, 1)
    kv_near(2, 0)
    kv_near(2, 1)
    tree(3, 0)
    tree(3, 1)
    kv_far(2, 0)
    kv_far(2, 1)
    kv_near(3, 0)
    kv_near(3, 1)
    tree(4, 0)
    tree(4, 1)
    z_mid_event()
    x_full(1)
    kv_far(3, 0)
    kv_far(3, 1)
    tree(5, 0)
    tree(5, 1)
    kv_near(4, 0)
    kv_near(4, 1)
    later[0].wait()
    res[...] = rest[...].T
    kv_far(4, 0)
    kv_far(4, 1)
    l_step(0)
    for copy in later[1:5]:
        copy.wait()
    prefix_pair(0)
    exchange_send(0, 0)
    z_last()
    prefix_pair(1)
    exchange_send(0, 1)
    l_step(1)
    x_full(2)
    exchange_relay(0, 0)
    exchange_relay(0, 1)
    l_step(2)
    exchange_forward(0, 0)
    exchange_forward(0, 1)
    l_step(3)
    x_half(0)
    x_half(1)
    l_step(4)
    option_pair(0)
    exchange_send(1, 0)
    option_pair(1)
    exchange_send(1, 1)
    x_full(3)
    exchange_rest(0, 0)
    exchange_rest(0, 1)
    exchange_relay(1, 0)
    exchange_relay(1, 1)
    exchange_forward(1, 0)
    exchange_forward(1, 1)
    exchange_rest(1, 0)
    exchange_rest(1, 1)
    project(0)
    project(1)
    x_half(2)
    project(2)
    for copy in later[5:]:
        copy.wait()
    x_half(3)
    project(3)

    square = jnp.sum(proj[...] * proj[...], axis=1, keepdims=True)
    diag = (
        lax.broadcasted_iota(jnp.int32, (128, 128), 0)
        == lax.broadcasted_iota(jnp.int32, (128, 128), 1)
    )
    row0 = jnp.sum(jnp.where(diag, square[0:128], 0.0), axis=0, keepdims=True)
    row1 = jnp.sum(jnp.where(diag[0:64], square[128:192], 0.0), axis=0, keepdims=True)
    ssq[head] = jnp.concatenate([row0, row1, jnp.zeros((6, 128), jnp.float32)], axis=0)
    mine = ssq.at[head]
    send(mine, mine, recv_id("sq0"), far)
    send(mine, mine, recv_id("sq1"), farsib)
    send(mine, mine, recv_id("sq2"), sib)
    drain()
    arrived(ssq.at[h_sib], recv_id("sq2"))
    arrived(ssq.at[h_far], recv_id("sq0"))
    arrived(ssq.at[h_farsib], recv_id("sq1"))
    total = ssq[0] + ssq[1] + ssq[2] + ssq[3]
    col0 = jnp.sum(jnp.where(diag, total[0:1], 0.0), axis=1, keepdims=True)
    col1 = jnp.sum(jnp.where(diag[0:64], total[1:2], 0.0), axis=1, keepdims=True)
    inv0 = lax.rsqrt(col0 / D + epsilon)
    inv1 = lax.rsqrt(col1 / D + epsilon)
    scale = gain[...].reshape(1, COLS)
    pout[...] = (
        (res[...].astype(jnp.float32) + proj[0:TOK, :] * inv0 * scale).astype(jnp.bfloat16).T
    )
    full = ores[...].astype(jnp.float32) + proj[TOK:ROWS, :] * inv1 * scale
    start = bounds[0, 0]
    length = bounds[0, 1]
    pos = lax.broadcasted_iota(jnp.int32, (OPT, COLS), 0)
    inside = pos < length
    out = jnp.where(inside, full, 0.0).astype(jnp.bfloat16)
    oout[...] = out
    chosen = inside & (pos >= start)
    picked = jnp.where(chosen, out.astype(jnp.float32), 0.0)
    count = jnp.broadcast_to((length - start).astype(jnp.float32), (1, COLS))
    osum[...] = jnp.sum(picked, axis=0, keepdims=True) / count
    drain()


def fused(*args):
    bf, f32 = jnp.bfloat16, jnp.float32
    anywhere = pl.BlockSpec(memory_space=pl.ANY)
    vmem = pl.BlockSpec(memory_space=pltpu.VMEM)
    return pl.pallas_call(
        kernel,
        out_shape=(
            jax.ShapeDtypeStruct((COLS, TOK), bf),
            jax.ShapeDtypeStruct((OPT, COLS), bf),
            jax.ShapeDtypeStruct((1, COLS), f32),
        ),
        in_specs=[anywhere] * 10 + [pl.BlockSpec(memory_space=pltpu.SMEM)],
        out_specs=(vmem, vmem, vmem),
        scratch_shapes=[
            pltpu.VMEM((TOK, 512), bf),
            pltpu.VMEM((OPT, 512), bf),
            pltpu.VMEM((OPT, 256), bf),
            pltpu.VMEM((OPT, 256), bf),
            pltpu.VMEM((COLS, TOK), bf),
            pltpu.VMEM((TOK, COLS), bf),
            pltpu.VMEM((OPT, COLS), bf),
            pltpu.VMEM((COLS,), f32),
            pltpu.VMEM((2, 9, TOK, 256), bf),
            pltpu.VMEM((2, 8, TOK, 256), bf),
            pltpu.VMEM((2048, COLS), bf),
            pltpu.VMEM((4, 2, ROWS, 256), bf),
            pltpu.VMEM((2, ROWS, 256), bf),
            pltpu.VMEM((ROWS, COLS), f32),
            pltpu.VMEM((4, 8, 128), f32),
            pltpu.SemaphoreType.DMA((16,)),
            pltpu.SemaphoreType.DMA((N_SEND,)),
            pltpu.SemaphoreType.DMA((N_RECV,)),
        ],
        compiler_params=pltpu.CompilerParams(
            collective_id=0, has_side_effects=True, vmem_limit_bytes=60 * 1024 * 1024
        ),
    )(*args)


def body(
    queries, keys, values, prefix_resid, opt_queries, opt_keys, opt_values, opt_resid,
    out_weight, norm_gain, option_bounds,
):
    prefix_out, option_out, option_summary = fused(
        queries, keys, values, prefix_resid.T, opt_queries[0], opt_keys[0], opt_values[0],
        opt_resid[0], out_weight, norm_gain, option_bounds,
    )
    return prefix_out.T, option_out[None], option_summary[None, 0]


def solution(mesh):
    return jax.shard_map(
        body,
        mesh=mesh,
        in_specs=(
            P("seq", "head"),
            P("seq", "head"),
            P("seq", "head"),
            P("seq", "head"),
            P("seq", None, "head"),
            P("seq", None, "head"),
            P("seq", None, "head"),
            P("seq", None, "head"),
            P("seq", "head"),
            P("head"),
            P("seq", None),
        ),
        out_specs=(P("seq", "head"), P("seq", None, "head"), P("seq", "head")),
        check_vma=False,
    )
```

```python
import jax
import jax.numpy as jnp
from jax import lax
from jax.experimental import pallas as pl
from jax.experimental.pallas import tpu as pltpu
from jax.sharding import PartitionSpec as P

D = 5376
HD = 128
WINDOW = 1024
TOK = 128
OPT = 64
COLS = 1344
NY = 8
ROWS = TOK + OPT
MESH = pl.DeviceIdType.MESH

score_scale = 168.0 ** (-0.5)
epsilon = 1e-06
exp2_scale = score_scale * 1.4426950408889634

N_RECV = 128
N_SEND = 224


def softmax_dot(scores, value_rows):
    top = jnp.max(scores, axis=1, keepdims=True)
    weights = jnp.exp2((scores - top) * exp2_scale)
    total = jnp.sum(weights, axis=1, keepdims=True)
    out = jnp.dot(weights.astype(jnp.bfloat16), value_rows, preferred_element_type=jnp.float32)
    return out / total


def score_dot(query_rows, key_rows):
    return lax.dot_general(
        query_rows, key_rows, (((1,), (1,)), ((), ())), preferred_element_type=jnp.float32
    )


def kernel(
    q_in, k_in, v_in, res_in, oq_in, ok_in, ov_in, ores_in, w_in, gain_in, bounds,
    pout, oout, osum,
    q, oq, ok, ov, rest, res, ores, gain, kv, lkv, wbuf, abuf, relay, proj, ssq,
    local_sem, send_sem, recv_sem,
):
    seq = lax.axis_index("seq")
    head = lax.axis_index("head")
    z = lax.div(seq, 32)
    x = lax.rem(lax.div(seq, 8), 4)
    y = lax.rem(seq, 8)
    zhi = lax.div(head, 2)
    core = lax.rem(head, 2)
    group = z * 4 + x

    def at(zz, xx, yy):
        return ((zz * 4 + xx) * 8 + yy, head)

    up_y = at(z, x, lax.rem(y + 1, 8))
    down_y = at(z, x, lax.rem(y + 7, 8))
    up_y2 = at(z, x, lax.rem(y + 2, 8))
    down_y2 = at(z, x, lax.rem(y + 6, 8))
    up_x = at(z, lax.rem(x + 1, 4), y)
    down_x = at(z, lax.rem(x + 3, 4), y)
    up_z = at(lax.rem(z + 1, 4), x, y)
    down_z = at(lax.rem(z + 3, 4), x, y)
    next_line = (lax.rem(seq + 8, 128), head)
    prev_line = (lax.rem(seq + 120, 128), head)
    h_sib = zhi * 2 + 1 - core
    h_far = (1 - zhi) * 2 + core
    h_farsib = (1 - zhi) * 2 + 1 - core
    sib = (seq, h_sib)
    far = (seq, h_far)
    farsib = (seq, h_farsib)
    z_mid = lax.rem(z + 2, 4)
    seq_mid = (z_mid * 4 + x) * 8 + y
    zhi_up = lax.rem(zhi + lax.div(z + 2, 4), 2)
    h_up = zhi_up * 2 + core
    h_down = (1 - zhi_up) * 2 + core
    mid_up = (seq_mid, h_up)
    mid_down = (seq_mid, h_down)

    local = []

    def load(src, dst, pred=None):
        copy = pltpu.make_async_copy(src, dst, local_sem.at[len(local)])
        local.append(copy)
        if pred is None:
            copy.start()
        else:
            pl.when(pred)(lambda: copy.start())
        return copy

    def rows16(g, yy):
        return wbuf.at[pl.ds(pl.multiple_of(g * 128 + yy * 16, 16), 16), :]

    def rows128(g):
        return wbuf.at[pl.ds(pl.multiple_of(g * 128, 128), 128), :]

    def rows64(g, half):
        return wbuf.at[pl.ds(pl.multiple_of(g * 128 + half * 64, 64), 64), :]

    is_source = (z == 3) & (x == 3)
    first = [
        load(w_in, rows16(group, y)),
        load(k_in, kv.at[0, 8]),
        load(v_in, kv.at[1, 8]),
    ]
    source_loads = [
        load(k_in, lkv.at[0, y], is_source),
        load(v_in, lkv.at[1, y], is_source),
    ]
    later = [
        load(res_in, rest),
        load(q_in, q), load(oq_in, oq), load(ok_in, ok), load(ov_in, ov),
        load(ores_in, ores), load(gain_in, gain),
    ]

    barrier = pltpu.get_barrier_semaphore()
    partners = [
        up_y, down_y, up_x, down_x, up_z, down_z, next_line, prev_line,
        sib, far, farsib, mid_up, mid_down, at(z_mid, x, y),
        up_y2, down_y2,
    ]
    for partner in partners:
        pl.semaphore_signal(barrier, inc=1, device_id=partner, device_id_type=MESH)
    for copy in first:
        copy.wait()

    @pl.when(is_source)
    def _():
        for copy in source_loads:
            copy.wait()

    pl.semaphore_wait(barrier, len(partners))

    sent = []
    n_sent = [0]
    received = {}

    def recv_id(name, count=1):
        if name not in received:
            received[name] = recv_id.next
            recv_id.next += count
            assert recv_id.next <= N_RECV
        return received[name]

    recv_id.next = 0

    def remote(src, dst, recv, device):
        n_sent[0] += 1
        assert n_sent[0] <= N_SEND
        return pltpu.make_async_remote_copy(
            src_ref=src, dst_ref=dst, send_sem=send_sem.at[n_sent[0] - 1],
            recv_sem=recv_sem.at[recv], device_id=device, device_id_type=MESH,
        )

    def send(src, dst, recv, device, pred=None):
        copy = remote(src, dst, recv, device)
        sent.append((copy, pred))
        if pred is None:
            copy.start()
        else:
            pl.when(pred)(lambda: copy.start())

    def arrived(ref, recv, pred=None):
        copy = pltpu.make_async_remote_copy(
            src_ref=ref, dst_ref=ref, send_sem=send_sem.at[0],
            recv_sem=recv_sem.at[recv], device_id=sib, device_id_type=MESH,
        )
        if pred is None:
            copy.wait_recv()
        else:
            pl.when(pred)(lambda: copy.wait_recv())

    def drain():
        for copy, pred in sent:
            if pred is None:
                copy.wait_send()
            else:
                pl.when(pred)(lambda copy=copy: copy.wait_send())
        sent.clear()

    def mod8(value):
        return lax.rem(value + 8, 8)

    zhalf = lax.div(z, 2)
    order = [
        z,
        z - 1 + 2 * (1 - lax.div(z + 3, 4)),
        2 + zhalf * (1 - 2 * lax.rem(z, 2)),
        3 * (1 - zhalf),
    ]
    wz = recv_id("wz", 4)
    xl = [recv_id(("xl", i)) for i in range(4)]
    xr = [recv_id(("xr", i)) for i in range(4)]
    hl = [recv_id(("hl", i)) for i in range(4)]
    hr = [recv_id(("hr", i)) for i in range(4)]

    def spread(piece):
        send(piece, piece, xl[0], up_x)
        send(piece, piece, xr[0], down_x)
        send(piece, piece, wz + z, up_z, z < 3)
        send(piece, piece, wz + z, down_z, z > 0)

    def wy_piece(d):
        return rows16(group, mod8(y - d))

    def wy_id(d):
        return recv_id(("wy", d))

    def wy_start():
        piece = wy_piece(0)
        send(piece, piece, wy_id(2), up_y2)
        send(piece, piece, wy_id(-2), down_y2)
        send(piece, piece, wy_id(1), up_y)
        send(piece, piece, wy_id(-1), down_y)
        spread(piece)

    def wy_take(d):
        piece = wy_piece(d)
        arrived(piece, wy_id(d))
        if d == 2:
            send(piece, piece, wy_id(3), up_y)
            send(piece, piece, wy_id(4), up_y2)
        if d == -2:
            send(piece, piece, wy_id(-3), down_y)
        spread(piece)

    inner = (z == 1) | (z == 2)

    def x_send(i):
        piece = rows128(order[i] * 4 + x)
        send(piece, piece, xl[i], up_x)
        send(piece, piece, xr[i], down_x)

    def z_take(i, pred=None):
        arrived(rows128(order[i] * 4 + x), wz + order[i], pred)

    def z_near():
        z_take(1)
        piece = rows128(order[1] * 4 + x)
        send(piece, piece, wz + order[1], up_z, (order[1] < z) & inner)
        x_send(1)
        z_take(2, inner)
        piece = rows128(order[2] * 4 + x)
        send(piece, piece, wz + order[2], down_z, (order[2] > z) & inner)

    def z_mid_event():
        z_take(2, (z == 0) | (z == 3))
        z_take(3, inner)
        piece = rows128(order[3] * 4 + x)
        send(piece, piece, wz + order[3], down_z, z == 1)
        send(piece, piece, wz + order[3], up_z, z == 2)
        x_send(2)

    def z_last():
        z_take(3, (z == 0) | (z == 3))
        x_send(3)

    def x_full(i):
        left = order[i] * 4 + lax.rem(x + 3, 4)
        right = order[i] * 4 + lax.rem(x + 1, 4)
        arrived(rows128(left), xl[i])
        send(rows64(left, 0), rows64(left, 0), hl[i], up_x)
        arrived(rows128(right), xr[i])
        send(rows64(right, 1), rows64(right, 1), hr[i], down_x)

    def x_half(i):
        across = order[i] * 4 + lax.rem(x + 2, 4)
        arrived(rows64(across, 0), hl[i])
        arrived(rows64(across, 1), hr[i])

    def kv_send(p, slot, to_slot, device, pred=None):
        send(kv.at[p, slot], kv.at[p, to_slot], recv_id(("kv", to_slot, p)), device, pred)

    def kv_wait(p, slot, pred=None):
        arrived(kv.at[p, slot], recv_id(("kv", slot, p)), pred)

    def kv_own(p):
        kv_send(p, 8, 7, up_y, y < 7)
        kv_send(p, 8, 0, next_line)
        kv_send(p, 8, 1, down_y, y == 0)
        kv_send(p, 8, 2, down_y2, y == 1)

    def kv_step(r, p):
        m = r - 1
        kv_wait(p, m, y <= 7 - m)
        if r == 1:
            kv_send(p, 0, 7, up_y, y == 7)
            kv_send(p, 0, 6, up_y2, y == 6)
        if r <= 4:
            kv_send(p, m, r, down_y, (y <= 7 - m) & (y > 0))
            kv_wait(p, 8 - r, y >= r)
            if r < 4:
                kv_send(p, 8 - r, 7 - r, up_y, (y >= r) & (y < 7))
            else:
                kv_send(p, 4, 3, up_y, y == 6)
        else:
            kv_send(p, 4, 5, down_y, y == 1)
            kv_wait(p, 3, y == 7)

    def kv_side(r, p):
        if r == 1:
            kv_wait(p, 1, y == 7)
            kv_send(p, 1, 2, down_y, y == 7)
            kv_wait(p, 2, y == 7)
            kv_send(p, 2, 3, down_y, y == 7)
        if r == 2:
            kv_wait(p, 2, y == 6)
            kv_send(p, 2, 3, down_y, y == 6)
            kv_wait(p, 7, y == 0)
            kv_send(p, 7, 6, up_y, y == 0)
            kv_wait(p, 6, y == 0)
            kv_send(p, 6, 5, up_y, y == 0)
        if r == 3:
            kv_wait(p, 3, y == 6)
            kv_wait(p, 3, y == 5)
            kv_wait(p, 6, y == 1)
            kv_send(p, 6, 5, up_y, y == 1)
            kv_wait(p, 5, y == 1)
        if r == 4:
            kv_wait(p, 5, y == 2)
        if r == 5:
            kv_wait(p, 5, y == 0)

    depth = lax.select(x == 3, 0, lax.select(x == 1, 2, 1)) + 3 - z
    tree_up = (z == 3) & ((x == 3) | (x == 0))
    tree_down = (z == 3) & (x == 3)
    tree_copies = []
    for p in range(2):
        piece = lkv.at[p, y]
        tree_id = recv_id(("tree", p))
        for device, pred in ((up_x, tree_up), (down_x, tree_down), (down_z, z > 0)):
            tree_copies.append((remote(piece, piece, tree_id, device), pred))
    sent.extend(tree_copies)

    def tree(k, p):
        here = depth == k
        if k:
            arrived(lkv.at[p, y], recv_id(("tree", p)), here)
        for copy, pred in tree_copies[3 * p:3 * p + 3]:
            pl.when(here & pred)(lambda copy=copy: copy.start())

    def l_up(k, p):
        last = 4 - p
        if k > last:
            return
        piece = lkv.at[p, mod8(y - k)]
        if k:
            arrived(piece, recv_id(("lp", k, p)))
        if k < last:
            send(piece, piece, recv_id(("lp", k + 1, p)), up_y)

    def l_down(k, p):
        last = 3 + p
        if k > last:
            return
        piece = lkv.at[p, lax.rem(y + k, 8)]
        if k:
            arrived(piece, recv_id(("lm", k, p)))
        if k < last:
            send(piece, piece, recv_id(("lm", k + 1, p)), down_y)

    def l_step(k):
        for p in range(2):
            l_up(k, p)
            l_down(k, p)

    def prefix_pair(i):
        keys = kv[0, :, :, i * HD:(i + 1) * HD].reshape(9 * TOK, HD)
        vals = kv[1, :, :, i * HD:(i + 1) * HD].reshape(9 * TOK, HD)
        for half in range(2):
            c = (2 * i + half) * HD
            scores = score_dot(q[:, c:c + HD], keys)
            row = lax.broadcasted_iota(jnp.int32, scores.shape, 0)
            col = lax.broadcasted_iota(jnp.int32, scores.shape, 1)
            allowed = (col > row) & (col <= row + WINDOW) & (col >= (8 - seq) * TOK)
            scores = jnp.where(allowed, scores, -jnp.inf)
            abuf[head, i, 0:TOK, half * HD:(half + 1) * HD] = softmax_dot(
                scores, vals
            ).astype(jnp.bfloat16)

    def option_pair(i):
        keys = lkv[0, :, :, i * HD:(i + 1) * HD].reshape(WINDOW, HD)
        vals = lkv[1, :, :, i * HD:(i + 1) * HD].reshape(WINDOW, HD)
        own_keys = ok[:, i * HD:(i + 1) * HD]
        own_vals = ov[:, i * HD:(i + 1) * HD]
        for half in range(2):
            c = (2 * i + half) * HD
            query = oq[:, c:c + HD]
            shared = score_dot(query, keys)
            own = score_dot(query, own_keys)
            row = lax.broadcasted_iota(jnp.int32, shared.shape, 0)
            col = lax.broadcasted_iota(jnp.int32, shared.shape, 1)
            shared = jnp.where(col > row, shared, -jnp.inf)
            row = lax.broadcasted_iota(jnp.int32, own.shape, 0)
            col = lax.broadcasted_iota(jnp.int32, own.shape, 1)
            own = jnp.where(col <= row, own, -jnp.inf)
            top = jnp.maximum(
                jnp.max(shared, axis=1, keepdims=True), jnp.max(own, axis=1, keepdims=True)
            )
            ws = jnp.exp2((shared - top) * exp2_scale)
            wo = jnp.exp2((own - top) * exp2_scale)
            total = jnp.sum(ws, axis=1, keepdims=True) + jnp.sum(wo, axis=1, keepdims=True)
            out = jnp.dot(ws.astype(jnp.bfloat16), vals, preferred_element_type=jnp.float32)
            out = out + jnp.dot(
                wo.astype(jnp.bfloat16), own_vals, preferred_element_type=jnp.float32
            )
            abuf[head, i, TOK:ROWS, half * HD:(half + 1) * HD] = (out / total).astype(
                jnp.bfloat16
            )

    def part_rows(part):
        return pl.ds(0, TOK) if part == 0 else pl.ds(TOK, OPT)

    def exchange_send(part, i):
        rows = part_rows(part)
        piece = abuf.at[head, i, rows, :]
        send(piece, relay.at[i, rows, :], recv_id(("mid", part, i)), (mid_up, mid_down)[i])
        send(piece, piece, recv_id(("sib", part, i)), sib)

    def exchange_relay(part, i):
        rows = part_rows(part)
        piece = relay.at[i, rows, :]
        arrived(piece, recv_id(("mid", part, i)))
        origin = (h_down, h_up)[i]
        send(
            piece, abuf.at[origin, i, rows, :], recv_id(("far", part, i)),
            (mid_up, mid_down)[i],
        )

    def exchange_forward(part, i):
        piece = abuf.at[h_far, i, part_rows(part), :]
        arrived(piece, recv_id(("far", part, i)))
        send(piece, piece, recv_id(("farsib", part, i)), sib)

    def exchange_sib(part):
        for i in range(2):
            arrived(abuf.at[h_sib, i, part_rows(part), :], recv_id(("sib", part, i)))

    def exchange_farsib(part):
        for i in range(2):
            arrived(abuf.at[h_farsib, i, part_rows(part), :], recv_id(("farsib", part, i)))

    def project(i):
        plane = (head, h_sib, h_far, h_farsib)[i]
        part = None
        for pair in range(2):
            rows = pl.ds(pl.multiple_of(plane * 512 + pair * 256, 256), 256)
            new = jnp.dot(
                abuf[plane, pair], wbuf[rows, :], preferred_element_type=jnp.float32
            )
            part = new if part is None else part + new
        if i == 0:
            proj[...] = part
        else:
            proj[...] += part

    wy_start()
    tree(0, 0)
    tree(0, 1)
    wy_take(2)
    wy_take(-2)
    kv_own(0)
    kv_own(1)
    wy_take(1)
    wy_take(-1)
    tree(1, 0)
    tree(1, 1)
    wy_take(3)
    wy_take(-3)
    wy_take(4)
    kv_step(1, 0)
    kv_step(1, 1)
    tree(2, 0)
    tree(2, 1)
    z_near()
    x_full(0)
    kv_side(1, 0)
    kv_side(1, 1)
    kv_step(2, 0)
    kv_step(2, 1)
    kv_side(2, 0)
    kv_side(2, 1)
    kv_step(3, 0)
    kv_step(3, 1)
    tree(3, 0)
    tree(3, 1)
    kv_side(3, 0)
    kv_side(3, 1)
    z_mid_event()
    x_full(1)
    tree(4, 0)
    tree(4, 1)
    kv_step(4, 0)
    kv_step(4, 1)
    kv_side(4, 0)
    kv_side(4, 1)
    tree(5, 0)
    tree(5, 1)
    l_step(0)
    kv_step(5, 0)
    kv_step(5, 1)
    kv_side(5, 0)
    kv_side(5, 1)
    for copy in later[1:5]:
        copy.wait()
    prefix_pair(0)
    exchange_send(0, 0)
    l_step(1)
    prefix_pair(1)
    exchange_send(0, 1)
    z_last()
    l_step(2)
    x_full(2)
    l_step(3)
    exchange_relay(0, 0)
    x_half(0)
    l_step(4)
    exchange_relay(0, 1)
    option_pair(0)
    exchange_send(1, 0)
    option_pair(1)
    exchange_send(1, 1)
    x_full(3)
    exchange_forward(0, 0)
    exchange_forward(0, 1)
    exchange_relay(1, 0)
    exchange_relay(1, 1)
    x_half(1)
    later[0].wait()
    res[...] = rest[...].T
    exchange_forward(1, 0)
    exchange_forward(1, 1)
    x_half(2)
    for copy in later[5:]:
        copy.wait()
    x_half(3)
    project(0)
    exchange_sib(0)
    exchange_sib(1)
    project(1)
    project(2)
    exchange_farsib(0)
    exchange_farsib(1)
    project(3)

    square = jnp.sum(proj[...] * proj[...], axis=1, keepdims=True)
    diag = (
        lax.broadcasted_iota(jnp.int32, (128, 128), 0)
        == lax.broadcasted_iota(jnp.int32, (128, 128), 1)
    )
    row0 = jnp.sum(jnp.where(diag, square[0:128], 0.0), axis=0, keepdims=True)
    row1 = jnp.sum(jnp.where(diag[0:64], square[128:192], 0.0), axis=0, keepdims=True)
    ssq[head] = jnp.concatenate([row0, row1, jnp.zeros((6, 128), jnp.float32)], axis=0)
    mine = ssq.at[head]
    send(mine, mine, recv_id("sq0"), far)
    send(mine, mine, recv_id("sq1"), farsib)
    send(mine, mine, recv_id("sq2"), sib)
    drain()
    arrived(ssq.at[h_sib], recv_id("sq2"))
    arrived(ssq.at[h_far], recv_id("sq0"))
    arrived(ssq.at[h_farsib], recv_id("sq1"))
    total = ssq[0] + ssq[1] + ssq[2] + ssq[3]
    col0 = jnp.sum(jnp.where(diag, total[0:1], 0.0), axis=1, keepdims=True)
    col1 = jnp.sum(jnp.where(diag[0:64], total[1:2], 0.0), axis=1, keepdims=True)
    inv0 = lax.rsqrt(col0 / D + epsilon)
    inv1 = lax.rsqrt(col1 / D + epsilon)
    scale = gain[...].reshape(1, COLS)
    pout[...] = (
        (res[...].astype(jnp.float32) + proj[0:TOK, :] * inv0 * scale).astype(jnp.bfloat16).T
    )
    full = ores[...].astype(jnp.float32) + proj[TOK:ROWS, :] * inv1 * scale
    start = bounds[0, 0]
    length = bounds[0, 1]
    pos = lax.broadcasted_iota(jnp.int32, (OPT, COLS), 0)
    inside = pos < length
    out = jnp.where(inside, full, 0.0).astype(jnp.bfloat16)
    oout[...] = out
    chosen = inside & (pos >= start)
    picked = jnp.where(chosen, out.astype(jnp.float32), 0.0)
    count = jnp.broadcast_to((length - start).astype(jnp.float32), (1, COLS))
    osum[...] = jnp.sum(picked, axis=0, keepdims=True) / count
    drain()


def fused(*args):
    bf, f32 = jnp.bfloat16, jnp.float32
    anywhere = pl.BlockSpec(memory_space=pl.ANY)
    vmem = pl.BlockSpec(memory_space=pltpu.VMEM)
    return pl.pallas_call(
        kernel,
        out_shape=(
            jax.ShapeDtypeStruct((COLS, TOK), bf),
            jax.ShapeDtypeStruct((OPT, COLS), bf),
            jax.ShapeDtypeStruct((1, COLS), f32),
        ),
        in_specs=[anywhere] * 10 + [pl.BlockSpec(memory_space=pltpu.SMEM)],
        out_specs=(vmem, vmem, vmem),
        scratch_shapes=[
            pltpu.VMEM((TOK, 512), bf),
            pltpu.VMEM((OPT, 512), bf),
            pltpu.VMEM((OPT, 256), bf),
            pltpu.VMEM((OPT, 256), bf),
            pltpu.VMEM((COLS, TOK), bf),
            pltpu.VMEM((TOK, COLS), bf),
            pltpu.VMEM((OPT, COLS), bf),
            pltpu.VMEM((COLS,), f32),
            pltpu.VMEM((2, 9, TOK, 256), bf),
            pltpu.VMEM((2, 8, TOK, 256), bf),
            pltpu.VMEM((2048, COLS), bf),
            pltpu.VMEM((4, 2, ROWS, 256), bf),
            pltpu.VMEM((2, ROWS, 256), bf),
            pltpu.VMEM((ROWS, COLS), f32),
            pltpu.VMEM((4, 8, 128), f32),
            pltpu.SemaphoreType.DMA((16,)),
            pltpu.SemaphoreType.DMA((N_SEND,)),
            pltpu.SemaphoreType.DMA((N_RECV,)),
        ],
        compiler_params=pltpu.CompilerParams(
            collective_id=0, has_side_effects=True, vmem_limit_bytes=60 * 1024 * 1024
        ),
    )(*args)


def body(
    queries, keys, values, prefix_resid, opt_queries, opt_keys, opt_values, opt_resid,
    out_weight, norm_gain, option_bounds,
):
    prefix_out, option_out, option_summary = fused(
        queries, keys, values, prefix_resid.T, opt_queries[0], opt_keys[0], opt_values[0],
        opt_resid[0], out_weight, norm_gain, option_bounds,
    )
    return prefix_out.T, option_out[None], option_summary[None, 0]


def solution(mesh):
    return jax.shard_map(
        body,
        mesh=mesh,
        in_specs=(
            P("seq", "head"),
            P("seq", "head"),
            P("seq", "head"),
            P("seq", "head"),
            P("seq", None, "head"),
            P("seq", None, "head"),
            P("seq", None, "head"),
            P("seq", None, "head"),
            P("seq", "head"),
            P("head"),
            P("seq", None),
        ),
        out_specs=(P("seq", "head"), P("seq", None, "head"), P("seq", "head")),
        check_vma=False,
    )
```

```python
import jax
import jax.numpy as jnp
from jax import lax
from jax.experimental import pallas as pl
from jax.experimental.pallas import tpu as pltpu
from jax.sharding import PartitionSpec as P

D = 5376
HD = 128
WINDOW = 1024
TOK = 128
OPT = 64
COLS = 1344
NY = 8
ROWS = TOK + OPT
MESH = pl.DeviceIdType.MESH

score_scale = 168.0 ** (-0.5)
epsilon = 1e-06
exp2_scale = score_scale * 1.4426950408889634

N_RECV = 128
N_SEND = 224


def softmax_dot(scores, value_rows):
    top = jnp.max(scores, axis=1, keepdims=True)
    weights = jnp.exp2((scores - top) * exp2_scale)
    total = jnp.sum(weights, axis=1, keepdims=True)
    out = jnp.dot(weights.astype(jnp.bfloat16), value_rows, preferred_element_type=jnp.float32)
    return out / total


def score_dot(query_rows, key_rows):
    return lax.dot_general(
        query_rows, key_rows, (((1,), (1,)), ((), ())), preferred_element_type=jnp.float32
    )


def kernel(
    q_in, k_in, v_in, res_in, oq_in, ok_in, ov_in, ores_in, w_in, gain_in, bounds,
    pout, oout, osum,
    q, oq, ok, ov, rest, res, ores, gain, kv, lkv, wbuf, abuf, relay, proj, ssq,
    local_sem, send_sem, recv_sem,
):
    seq = lax.axis_index("seq")
    head = lax.axis_index("head")
    z = lax.div(seq, 32)
    x = lax.rem(lax.div(seq, 8), 4)
    y = lax.rem(seq, 8)
    zhi = lax.div(head, 2)
    core = lax.rem(head, 2)
    group = z * 4 + x

    def at(zz, xx, yy):
        return ((zz * 4 + xx) * 8 + yy, head)

    up_y = at(z, x, lax.rem(y + 1, 8))
    down_y = at(z, x, lax.rem(y + 7, 8))
    up_y2 = at(z, x, lax.rem(y + 2, 8))
    down_y2 = at(z, x, lax.rem(y + 6, 8))
    up_x = at(z, lax.rem(x + 1, 4), y)
    down_x = at(z, lax.rem(x + 3, 4), y)
    up_z = at(lax.rem(z + 1, 4), x, y)
    down_z = at(lax.rem(z + 3, 4), x, y)
    next_line = (lax.rem(seq + 8, 128), head)
    prev_line = (lax.rem(seq + 120, 128), head)
    h_sib = zhi * 2 + 1 - core
    h_far = (1 - zhi) * 2 + core
    h_farsib = (1 - zhi) * 2 + 1 - core
    sib = (seq, h_sib)
    far = (seq, h_far)
    farsib = (seq, h_farsib)
    z_mid = lax.rem(z + 2, 4)
    seq_mid = (z_mid * 4 + x) * 8 + y
    zhi_up = lax.rem(zhi + lax.div(z + 2, 4), 2)
    h_up = zhi_up * 2 + core
    h_down = (1 - zhi_up) * 2 + core
    mid_up = (seq_mid, h_up)
    mid_down = (seq_mid, h_down)

    local = []

    def load(src, dst, pred=None):
        copy = pltpu.make_async_copy(src, dst, local_sem.at[len(local)])
        local.append(copy)
        if pred is None:
            copy.start()
        else:
            pl.when(pred)(lambda: copy.start())
        return copy

    def rows16(g, yy):
        return wbuf.at[pl.ds(pl.multiple_of(g * 128 + yy * 16, 16), 16), :]

    def rows128(g):
        return wbuf.at[pl.ds(pl.multiple_of(g * 128, 128), 128), :]

    def rows64(g, half):
        return wbuf.at[pl.ds(pl.multiple_of(g * 128 + half * 64, 64), 64), :]

    is_source = (z == 3) & (x == 3)
    first = [
        load(w_in, rows16(group, y)),
        load(k_in, kv.at[0, 8]),
        load(v_in, kv.at[1, 8]),
    ]
    source_loads = [
        load(k_in, lkv.at[0, y], is_source),
        load(v_in, lkv.at[1, y], is_source),
    ]
    later = [
        load(res_in, rest),
        load(q_in, q), load(oq_in, oq), load(ok_in, ok), load(ov_in, ov),
        load(ores_in, ores), load(gain_in, gain),
    ]

    barrier = pltpu.get_barrier_semaphore()
    partners = [
        up_y, down_y, up_x, down_x, up_z, down_z, next_line, prev_line,
        sib, far, farsib, mid_up, mid_down,
        up_y2, down_y2,
    ]
    for partner in partners:
        pl.semaphore_signal(barrier, inc=1, device_id=partner, device_id_type=MESH)
    for copy in first:
        copy.wait()

    @pl.when(is_source)
    def _():
        for copy in source_loads:
            copy.wait()

    pl.semaphore_wait(barrier, len(partners))

    sent = []
    n_sent = [0]
    received = {}

    def recv_id(name, count=1):
        if name not in received:
            received[name] = recv_id.next
            recv_id.next += count
            assert recv_id.next <= N_RECV
        return received[name]

    recv_id.next = 0

    def remote(src, dst, recv, device):
        n_sent[0] += 1
        assert n_sent[0] <= N_SEND
        return pltpu.make_async_remote_copy(
            src_ref=src, dst_ref=dst, send_sem=send_sem.at[n_sent[0] - 1],
            recv_sem=recv_sem.at[recv], device_id=device, device_id_type=MESH,
        )

    def send(src, dst, recv, device, pred=None):
        copy = remote(src, dst, recv, device)
        sent.append((copy, pred))
        if pred is None:
            copy.start()
        else:
            pl.when(pred)(lambda: copy.start())

    def arrived(ref, recv, pred=None):
        copy = pltpu.make_async_remote_copy(
            src_ref=ref, dst_ref=ref, send_sem=send_sem.at[0],
            recv_sem=recv_sem.at[recv], device_id=sib, device_id_type=MESH,
        )
        if pred is None:
            copy.wait_recv()
        else:
            pl.when(pred)(lambda: copy.wait_recv())

    def drain():
        for copy, pred in sent:
            if pred is None:
                copy.wait_send()
            else:
                pl.when(pred)(lambda copy=copy: copy.wait_send())
        sent.clear()

    def mod8(value):
        return lax.rem(value + 8, 8)

    zhalf = lax.div(z, 2)
    order = [
        z,
        z - 1 + 2 * (1 - lax.div(z + 3, 4)),
        2 + zhalf * (1 - 2 * lax.rem(z, 2)),
        3 * (1 - zhalf),
    ]
    wz = recv_id("wz", 4)
    xl = [recv_id(("xl", i)) for i in range(4)]
    xr = [recv_id(("xr", i)) for i in range(4)]
    hl = [recv_id(("hl", i)) for i in range(4)]
    hr = [recv_id(("hr", i)) for i in range(4)]

    def spread(piece):
        send(piece, piece, xl[0], up_x)
        send(piece, piece, xr[0], down_x)
        send(piece, piece, wz + z, up_z, z < 3)
        send(piece, piece, wz + z, down_z, z > 0)

    def wy_piece(d):
        return rows16(group, mod8(y - d))

    def wy_id(d):
        return recv_id(("wy", d))

    def wy_start():
        piece = wy_piece(0)
        send(piece, piece, wy_id(2), up_y2)
        send(piece, piece, wy_id(-2), down_y2)
        send(piece, piece, wy_id(1), up_y)
        send(piece, piece, wy_id(-1), down_y)
        spread(piece)

    def wy_take(d):
        piece = wy_piece(d)
        arrived(piece, wy_id(d))
        if d == 2:
            send(piece, piece, wy_id(3), up_y)
            send(piece, piece, wy_id(4), up_y2)
        if d == -2:
            send(piece, piece, wy_id(-3), down_y)
        spread(piece)

    inner = (z == 1) | (z == 2)

    def x_send(i):
        piece = rows128(order[i] * 4 + x)
        send(piece, piece, xl[i], up_x)
        send(piece, piece, xr[i], down_x)

    def z_take(i, pred=None):
        arrived(rows128(order[i] * 4 + x), wz + order[i], pred)

    def z_near():
        z_take(1)
        piece = rows128(order[1] * 4 + x)
        send(piece, piece, wz + order[1], up_z, (order[1] < z) & inner)
        x_send(1)
        z_take(2, inner)
        piece = rows128(order[2] * 4 + x)
        send(piece, piece, wz + order[2], down_z, (order[2] > z) & inner)

    def z_mid_event():
        z_take(2, (z == 0) | (z == 3))
        z_take(3, inner)
        piece = rows128(order[3] * 4 + x)
        send(piece, piece, wz + order[3], down_z, z == 1)
        send(piece, piece, wz + order[3], up_z, z == 2)
        x_send(2)

    def z_last():
        z_take(3, (z == 0) | (z == 3))
        x_send(3)

    def x_full(i):
        left = order[i] * 4 + lax.rem(x + 3, 4)
        right = order[i] * 4 + lax.rem(x + 1, 4)
        arrived(rows128(left), xl[i])
        send(rows64(left, 0), rows64(left, 0), hl[i], up_x)
        arrived(rows128(right), xr[i])
        send(rows64(right, 1), rows64(right, 1), hr[i], down_x)

    def x_half(i):
        across = order[i] * 4 + lax.rem(x + 2, 4)
        arrived(rows64(across, 0), hl[i])
        arrived(rows64(across, 1), hr[i])

    def kv_send(p, slot, to_slot, device, pred=None):
        send(kv.at[p, slot], kv.at[p, to_slot], recv_id(("kv", to_slot, p)), device, pred)

    def kv_wait(p, slot, pred=None):
        arrived(kv.at[p, slot], recv_id(("kv", slot, p)), pred)

    def kv_own(p):
        kv_send(p, 8, 7, up_y, y < 7)
        kv_send(p, 8, 0, next_line)
        kv_send(p, 8, 1, down_y, y == 0)
        kv_send(p, 8, 2, down_y2, y == 1)

    def kv_step(r, p):
        m = r - 1
        kv_wait(p, m, y <= 7 - m)
        if r == 1:
            kv_send(p, 0, 7, up_y, y == 7)
            kv_send(p, 0, 6, up_y2, y == 6)
        if r <= 4:
            kv_send(p, m, r, down_y, (y <= 7 - m) & (y > 0))
            kv_wait(p, 8 - r, y >= r)
            if r < 4:
                kv_send(p, 8 - r, 7 - r, up_y, (y >= r) & (y < 7))
            else:
                kv_send(p, 4, 3, up_y, y == 6)
        else:
            kv_send(p, 4, 5, down_y, y == 1)
            kv_wait(p, 3, y == 7)

    def kv_side(r, p):
        if r == 1:
            kv_wait(p, 1, y == 7)
            kv_send(p, 1, 2, down_y, y == 7)
            kv_wait(p, 2, y == 7)
            kv_send(p, 2, 3, down_y, y == 7)
        if r == 2:
            kv_wait(p, 2, y == 6)
            kv_send(p, 2, 3, down_y, y == 6)
            kv_wait(p, 7, y == 0)
            kv_send(p, 7, 6, up_y, y == 0)
            kv_wait(p, 6, y == 0)
            kv_send(p, 6, 5, up_y, y == 0)
        if r == 3:
            kv_wait(p, 3, y == 6)
            kv_wait(p, 3, y == 5)
            kv_wait(p, 6, y == 1)
            kv_send(p, 6, 5, up_y, y == 1)
            kv_wait(p, 5, y == 1)
        if r == 4:
            kv_wait(p, 5, y == 2)
        if r == 5:
            kv_wait(p, 5, y == 0)

    depth = lax.select(x == 3, 0, lax.select(x == 1, 2, 1)) + 3 - z
    tree_up = (z == 3) & ((x == 3) | (x == 0))
    tree_down = (z == 3) & (x == 3)
    tree_copies = []
    for p in range(2):
        piece = lkv.at[p, y]
        tree_id = recv_id(("tree", p))
        for device, pred in ((up_x, tree_up), (down_x, tree_down), (down_z, z > 0)):
            tree_copies.append((remote(piece, piece, tree_id, device), pred))
    sent.extend(tree_copies)

    def tree(k, p):
        here = depth == k
        if k:
            arrived(lkv.at[p, y], recv_id(("tree", p)), here)
        for copy, pred in tree_copies[3 * p:3 * p + 3]:
            pl.when(here & pred)(lambda copy=copy: copy.start())

    def l_up(k, p):
        last = 4 - p
        if k > last:
            return
        piece = lkv.at[p, mod8(y - k)]
        if k:
            arrived(piece, recv_id(("lp", k, p)))
        if k < last:
            send(piece, piece, recv_id(("lp", k + 1, p)), up_y)

    def l_down(k, p):
        last = 3 + p
        if k > last:
            return
        piece = lkv.at[p, lax.rem(y + k, 8)]
        if k:
            arrived(piece, recv_id(("lm", k, p)))
        if k < last:
            send(piece, piece, recv_id(("lm", k + 1, p)), down_y)

    def l_step(k):
        for p in range(2):
            l_up(k, p)
            l_down(k, p)

    def prefix_pair(i):
        keys = kv[0, :, :, i * HD:(i + 1) * HD].reshape(9 * TOK, HD)
        vals = kv[1, :, :, i * HD:(i + 1) * HD].reshape(9 * TOK, HD)
        for half in range(2):
            c = (2 * i + half) * HD
            scores = score_dot(q[:, c:c + HD], keys)
            row = lax.broadcasted_iota(jnp.int32, scores.shape, 0)
            col = lax.broadcasted_iota(jnp.int32, scores.shape, 1)
            allowed = (col > row) & (col <= row + WINDOW) & (col >= (8 - seq) * TOK)
            scores = jnp.where(allowed, scores, -jnp.inf)
            abuf[head, i, 0:TOK, half * HD:(half + 1) * HD] = softmax_dot(
                scores, vals
            ).astype(jnp.bfloat16)

    def option_pair(i):
        keys = lkv[0, :, :, i * HD:(i + 1) * HD].reshape(WINDOW, HD)
        vals = lkv[1, :, :, i * HD:(i + 1) * HD].reshape(WINDOW, HD)
        own_keys = ok[:, i * HD:(i + 1) * HD]
        own_vals = ov[:, i * HD:(i + 1) * HD]
        for half in range(2):
            c = (2 * i + half) * HD
            query = oq[:, c:c + HD]
            shared = score_dot(query, keys)
            own = score_dot(query, own_keys)
            row = lax.broadcasted_iota(jnp.int32, shared.shape, 0)
            col = lax.broadcasted_iota(jnp.int32, shared.shape, 1)
            shared = jnp.where(col > row, shared, -jnp.inf)
            row = lax.broadcasted_iota(jnp.int32, own.shape, 0)
            col = lax.broadcasted_iota(jnp.int32, own.shape, 1)
            own = jnp.where(col <= row, own, -jnp.inf)
            top = jnp.maximum(
                jnp.max(shared, axis=1, keepdims=True), jnp.max(own, axis=1, keepdims=True)
            )
            ws = jnp.exp2((shared - top) * exp2_scale)
            wo = jnp.exp2((own - top) * exp2_scale)
            total = jnp.sum(ws, axis=1, keepdims=True) + jnp.sum(wo, axis=1, keepdims=True)
            out = jnp.dot(ws.astype(jnp.bfloat16), vals, preferred_element_type=jnp.float32)
            out = out + jnp.dot(
                wo.astype(jnp.bfloat16), own_vals, preferred_element_type=jnp.float32
            )
            abuf[head, i, TOK:ROWS, half * HD:(half + 1) * HD] = (out / total).astype(
                jnp.bfloat16
            )

    def part_rows(part):
        return pl.ds(0, TOK) if part == 0 else pl.ds(TOK, OPT)

    def exchange_send(part, i):
        rows = part_rows(part)
        piece = abuf.at[head, i, rows, :]
        send(piece, relay.at[i, rows, :], recv_id(("mid", part, i)), (mid_up, mid_down)[i])
        send(piece, piece, recv_id(("sib", part, i)), sib)

    def exchange_relay(part, i):
        rows = part_rows(part)
        piece = relay.at[i, rows, :]
        arrived(piece, recv_id(("mid", part, i)))
        origin = (h_down, h_up)[i]
        send(
            piece, abuf.at[origin, i, rows, :], recv_id(("far", part, i)),
            (mid_up, mid_down)[i],
        )

    def exchange_forward(part, i):
        piece = abuf.at[h_far, i, part_rows(part), :]
        arrived(piece, recv_id(("far", part, i)))
        send(piece, piece, recv_id(("farsib", part, i)), sib)

    def exchange_sib(part):
        for i in range(2):
            arrived(abuf.at[h_sib, i, part_rows(part), :], recv_id(("sib", part, i)))

    def exchange_farsib(part):
        for i in range(2):
            arrived(abuf.at[h_farsib, i, part_rows(part), :], recv_id(("farsib", part, i)))

    def project(i):
        plane = (head, h_sib, h_far, h_farsib)[i]
        part = None
        for pair in range(2):
            rows = pl.ds(pl.multiple_of(plane * 512 + pair * 256, 256), 256)
            new = jnp.dot(
                abuf[plane, pair], wbuf[rows, :], preferred_element_type=jnp.float32
            )
            part = new if part is None else part + new
        if i == 0:
            proj[...] = part
        else:
            proj[...] += part

    wy_start()
    tree(0, 0)
    tree(0, 1)
    wy_take(2)
    wy_take(-2)
    kv_own(0)
    kv_own(1)
    wy_take(1)
    wy_take(-1)
    tree(1, 0)
    tree(1, 1)
    wy_take(3)
    wy_take(-3)
    wy_take(4)
    kv_step(1, 0)
    kv_step(1, 1)
    tree(2, 0)
    tree(2, 1)
    later[0].wait()
    res[...] = rest[...].T
    z_near()
    x_full(0)
    kv_side(1, 0)
    kv_side(1, 1)
    kv_step(2, 0)
    kv_step(2, 1)
    kv_side(2, 0)
    kv_side(2, 1)
    kv_step(3, 0)
    kv_step(3, 1)
    tree(3, 0)
    tree(3, 1)
    kv_side(3, 0)
    kv_side(3, 1)
    z_mid_event()
    x_full(1)
    tree(4, 0)
    tree(4, 1)
    kv_step(4, 0)
    kv_step(4, 1)
    kv_side(4, 0)
    kv_side(4, 1)
    tree(5, 0)
    tree(5, 1)
    l_step(0)
    kv_step(5, 0)
    kv_step(5, 1)
    kv_side(5, 0)
    kv_side(5, 1)
    for copy in later[1:5]:
        copy.wait()
    prefix_pair(0)
    exchange_send(0, 0)
    l_step(1)
    prefix_pair(1)
    exchange_send(0, 1)
    z_last()
    l_step(2)
    x_full(2)
    l_step(3)
    exchange_relay(0, 0)
    x_half(0)
    l_step(4)
    exchange_relay(0, 1)
    option_pair(0)
    exchange_send(1, 0)
    option_pair(1)
    exchange_send(1, 1)
    x_full(3)
    exchange_forward(0, 0)
    exchange_forward(0, 1)
    exchange_relay(1, 0)
    exchange_relay(1, 1)
    x_half(1)
    exchange_forward(1, 0)
    exchange_forward(1, 1)
    x_half(2)
    for copy in later[5:]:
        copy.wait()
    x_half(3)
    project(0)
    exchange_sib(0)
    exchange_sib(1)
    project(1)
    project(2)
    exchange_farsib(0)
    exchange_farsib(1)
    project(3)

    square = jnp.sum(proj[...] * proj[...], axis=1, keepdims=True)
    diag = (
        lax.broadcasted_iota(jnp.int32, (128, 128), 0)
        == lax.broadcasted_iota(jnp.int32, (128, 128), 1)
    )
    row0 = jnp.sum(jnp.where(diag, square[0:128], 0.0), axis=0, keepdims=True)
    row1 = jnp.sum(jnp.where(diag[0:64], square[128:192], 0.0), axis=0, keepdims=True)
    ssq[head] = jnp.concatenate([row0, row1, jnp.zeros((6, 128), jnp.float32)], axis=0)
    mine = ssq.at[head]
    send(mine, mine, recv_id("sq0"), far)
    send(mine, mine, recv_id("sq1"), farsib)
    send(mine, mine, recv_id("sq2"), sib)
    drain()
    arrived(ssq.at[h_sib], recv_id("sq2"))
    arrived(ssq.at[h_far], recv_id("sq0"))
    arrived(ssq.at[h_farsib], recv_id("sq1"))
    total = ssq[0] + ssq[1] + ssq[2] + ssq[3]
    col0 = jnp.sum(jnp.where(diag, total[0:1], 0.0), axis=1, keepdims=True)
    col1 = jnp.sum(jnp.where(diag[0:64], total[1:2], 0.0), axis=1, keepdims=True)
    inv0 = lax.rsqrt(col0 / D + epsilon)
    inv1 = lax.rsqrt(col1 / D + epsilon)
    scale = gain[...].reshape(1, COLS)
    pout[...] = (
        (res[...].astype(jnp.float32) + proj[0:TOK, :] * inv0 * scale).astype(jnp.bfloat16).T
    )
    full = ores[...].astype(jnp.float32) + proj[TOK:ROWS, :] * inv1 * scale
    start = bounds[0, 0]
    length = bounds[0, 1]
    pos = lax.broadcasted_iota(jnp.int32, (OPT, COLS), 0)
    inside = pos < length
    out = jnp.where(inside, full, 0.0).astype(jnp.bfloat16)
    oout[...] = out
    chosen = inside & (pos >= start)
    picked = jnp.where(chosen, out.astype(jnp.float32), 0.0)
    count = jnp.broadcast_to((length - start).astype(jnp.float32), (1, COLS))
    osum[...] = jnp.sum(picked, axis=0, keepdims=True) / count
    drain()


def fused(*args):
    bf, f32 = jnp.bfloat16, jnp.float32
    vmem = pl.BlockSpec(memory_space=pltpu.VMEM)
    return pl.pallas_call(
        kernel,
        out_shape=(
            jax.ShapeDtypeStruct((COLS, TOK), bf),
            jax.ShapeDtypeStruct((OPT, COLS), bf),
            jax.ShapeDtypeStruct((1, COLS), f32),
        ),
        in_specs=[pl.BlockSpec(memory_space=pltpu.HBM)] * 10
        + [pl.BlockSpec(memory_space=pltpu.SMEM)],
        out_specs=(vmem, vmem, vmem),
        scratch_shapes=[
            pltpu.VMEM((TOK, 512), bf),
            pltpu.VMEM((OPT, 512), bf),
            pltpu.VMEM((OPT, 256), bf),
            pltpu.VMEM((OPT, 256), bf),
            pltpu.VMEM((COLS, TOK), bf),
            pltpu.VMEM((TOK, COLS), bf),
            pltpu.VMEM((OPT, COLS), bf),
            pltpu.VMEM((COLS,), f32),
            pltpu.VMEM((2, 9, TOK, 256), bf),
            pltpu.VMEM((2, 8, TOK, 256), bf),
            pltpu.VMEM((2048, COLS), bf),
            pltpu.VMEM((4, 2, ROWS, 256), bf),
            pltpu.VMEM((2, ROWS, 256), bf),
            pltpu.VMEM((ROWS, COLS), f32),
            pltpu.VMEM((4, 8, 128), f32),
            pltpu.SemaphoreType.DMA((16,)),
            pltpu.SemaphoreType.DMA((N_SEND,)),
            pltpu.SemaphoreType.DMA((N_RECV,)),
        ],
        compiler_params=pltpu.CompilerParams(
            collective_id=0, has_side_effects=True, vmem_limit_bytes=60 * 1024 * 1024
        ),
    )(*args)


def write_kernel(a_in, b_in, c_in, a_out, b_out, c_out, a, b, c, sems):
    ways = [(a_in, a, a_out), (b_in, b, b_out), (c_in, c, c_out)]
    reads = [pltpu.make_async_copy(w[0], w[1], sems.at[i]) for i, w in enumerate(ways)]
    writes = [pltpu.make_async_copy(w[1], w[2], sems.at[3 + i]) for i, w in enumerate(ways)]
    for read in reads:
        read.start()
    for read, write in zip(reads, writes):
        read.wait()
        write.start()
    for write in writes:
        write.wait()


def written(*results):
    hbm = pl.BlockSpec(memory_space=pltpu.HBM)
    return pl.pallas_call(
        write_kernel,
        out_shape=tuple(jax.ShapeDtypeStruct(r.shape, r.dtype) for r in results),
        in_specs=[hbm] * 3,
        out_specs=(hbm,) * 3,
        scratch_shapes=[pltpu.VMEM(r.shape, r.dtype) for r in results]
        + [pltpu.SemaphoreType.DMA((6,))],
        compiler_params=pltpu.CompilerParams(vmem_limit_bytes=60 * 1024 * 1024),
    )(*results)


def body(
    queries, keys, values, prefix_resid, opt_queries, opt_keys, opt_values, opt_resid,
    out_weight, norm_gain, option_bounds,
):
    prefix_out, option_out, option_summary = fused(
        queries, keys, values, prefix_resid.T, opt_queries[0], opt_keys[0], opt_values[0],
        opt_resid[0], out_weight, norm_gain, option_bounds,
    )
    prefix_out, option_out, option_summary = written(prefix_out, option_out, option_summary)
    return prefix_out.T, option_out[None], option_summary[None, 0]


def solution(mesh):
    return jax.shard_map(
        body,
        mesh=mesh,
        in_specs=(
            P("seq", "head"),
            P("seq", "head"),
            P("seq", "head"),
            P("seq", "head"),
            P("seq", None, "head"),
            P("seq", None, "head"),
            P("seq", None, "head"),
            P("seq", None, "head"),
            P("seq", "head"),
            P("head"),
            P("seq", None),
        ),
        out_specs=(P("seq", "head"), P("seq", None, "head"), P("seq", "head")),
        check_vma=False,
    )
```

```python
import jax
import jax.numpy as jnp
from jax import lax
from jax.experimental import pallas as pl
from jax.experimental.pallas import tpu as pltpu
from jax.sharding import PartitionSpec as P

D = 5376
HD = 128
WINDOW = 1024
TOK = 128
OPT = 64
COLS = 1344
NY = 8
ROWS = TOK + OPT
MESH = pl.DeviceIdType.MESH

score_scale = 168.0 ** (-0.5)
epsilon = 1e-06
exp2_scale = score_scale * 1.4426950408889634

N_RECV = 128
N_SEND = 224


def softmax_dot(scores, value_rows):
    top = jnp.max(scores, axis=1, keepdims=True)
    weights = jnp.exp2((scores - top) * exp2_scale)
    total = jnp.sum(weights, axis=1, keepdims=True)
    out = jnp.dot(weights.astype(jnp.bfloat16), value_rows, preferred_element_type=jnp.float32)
    return out / total


def score_dot(query_rows, key_rows):
    return lax.dot_general(
        query_rows, key_rows, (((1,), (1,)), ((), ())), preferred_element_type=jnp.float32
    )


def kernel(
    q_in, k_in, v_in, res_in, oq_in, ok_in, ov_in, ores_in, w_in, gain_in, bounds,
    pout, oout, osum,
    q, oq, ok, ov, rest, res, ores, gain, kv, lkv, wbuf, abuf, relay, proj, ssq,
    local_sem, send_sem, recv_sem,
):
    seq = lax.axis_index("seq")
    head = lax.axis_index("head")
    z = lax.div(seq, 32)
    x = lax.rem(lax.div(seq, 8), 4)
    y = lax.rem(seq, 8)
    zhi = lax.div(head, 2)
    core = lax.rem(head, 2)
    group = z * 4 + x

    def at(zz, xx, yy):
        return ((zz * 4 + xx) * 8 + yy, head)

    up_y = at(z, x, lax.rem(y + 1, 8))
    down_y = at(z, x, lax.rem(y + 7, 8))
    up_y2 = at(z, x, lax.rem(y + 2, 8))
    down_y2 = at(z, x, lax.rem(y + 6, 8))
    up_x = at(z, lax.rem(x + 1, 4), y)
    down_x = at(z, lax.rem(x + 3, 4), y)
    up_z = at(lax.rem(z + 1, 4), x, y)
    down_z = at(lax.rem(z + 3, 4), x, y)
    next_line = (lax.rem(seq + 8, 128), head)
    prev_line = (lax.rem(seq + 120, 128), head)
    h_sib = zhi * 2 + 1 - core
    h_far = (1 - zhi) * 2 + core
    h_farsib = (1 - zhi) * 2 + 1 - core
    sib = (seq, h_sib)
    far = (seq, h_far)
    farsib = (seq, h_farsib)
    z_mid = lax.rem(z + 2, 4)
    seq_mid = (z_mid * 4 + x) * 8 + y
    zhi_up = lax.rem(zhi + lax.div(z + 2, 4), 2)
    h_up = zhi_up * 2 + core
    h_down = (1 - zhi_up) * 2 + core
    mid_up = (seq_mid, h_up)
    mid_down = (seq_mid, h_down)

    local = []

    def load(src, dst, pred=None):
        copy = pltpu.make_async_copy(src, dst, local_sem.at[len(local)])
        local.append(copy)
        if pred is None:
            copy.start()
        else:
            pl.when(pred)(lambda: copy.start())
        return copy

    def rows16(g, yy):
        return wbuf.at[pl.ds(pl.multiple_of(g * 128 + yy * 16, 16), 16), :]

    def rows128(g):
        return wbuf.at[pl.ds(pl.multiple_of(g * 128, 128), 128), :]

    def rows64(g, half):
        return wbuf.at[pl.ds(pl.multiple_of(g * 128 + half * 64, 64), 64), :]

    is_source = (z == 3) & (x == 3)
    first = [
        load(w_in, rows16(group, y)),
        load(k_in, kv.at[0, 8]),
        load(v_in, kv.at[1, 8]),
    ]
    source_loads = [
        load(k_in, lkv.at[0, y], is_source),
        load(v_in, lkv.at[1, y], is_source),
    ]
    later = [
        load(res_in, rest),
        load(q_in, q), load(oq_in, oq), load(ok_in, ok), load(ov_in, ov),
        load(ores_in, ores), load(gain_in, gain),
    ]

    barrier = pltpu.get_barrier_semaphore()
    partners = [
        up_y, down_y, up_x, down_x, up_z, down_z, next_line, prev_line,
        sib, far, farsib, mid_up, mid_down,
        up_y2, down_y2,
    ]
    for partner in partners:
        pl.semaphore_signal(barrier, inc=1, device_id=partner, device_id_type=MESH)
    for copy in first:
        copy.wait()

    @pl.when(is_source)
    def _():
        for copy in source_loads:
            copy.wait()

    pl.semaphore_wait(barrier, len(partners))

    sent = []
    n_sent = [0]
    received = {}

    def recv_id(name, count=1):
        if name not in received:
            received[name] = recv_id.next
            recv_id.next += count
            assert recv_id.next <= N_RECV
        return received[name]

    recv_id.next = 0

    def remote(src, dst, recv, device):
        n_sent[0] += 1
        assert n_sent[0] <= N_SEND
        return pltpu.make_async_remote_copy(
            src_ref=src, dst_ref=dst, send_sem=send_sem.at[n_sent[0] - 1],
            recv_sem=recv_sem.at[recv], device_id=device, device_id_type=MESH,
        )

    def send(src, dst, recv, device, pred=None):
        copy = remote(src, dst, recv, device)
        sent.append((copy, pred))
        if pred is None:
            copy.start()
        else:
            pl.when(pred)(lambda: copy.start())

    def arrived(ref, recv, pred=None):
        copy = pltpu.make_async_remote_copy(
            src_ref=ref, dst_ref=ref, send_sem=send_sem.at[0],
            recv_sem=recv_sem.at[recv], device_id=sib, device_id_type=MESH,
        )
        if pred is None:
            copy.wait_recv()
        else:
            pl.when(pred)(lambda: copy.wait_recv())

    def drain():
        for copy, pred in sent:
            if pred is None:
                copy.wait_send()
            else:
                pl.when(pred)(lambda copy=copy: copy.wait_send())
        sent.clear()

    def mod8(value):
        return lax.rem(value + 8, 8)

    zhalf = lax.div(z, 2)
    order = [
        z,
        z - 1 + 2 * (1 - lax.div(z + 3, 4)),
        2 + zhalf * (1 - 2 * lax.rem(z, 2)),
        3 * (1 - zhalf),
    ]
    wz = recv_id("wz", 4)
    xl = [recv_id(("xl", i)) for i in range(4)]
    xr = [recv_id(("xr", i)) for i in range(4)]
    hl = [recv_id(("hl", i)) for i in range(4)]
    hr = [recv_id(("hr", i)) for i in range(4)]

    def spread(piece):
        send(piece, piece, xl[0], up_x)
        send(piece, piece, xr[0], down_x)
        send(piece, piece, wz + z, up_z, z < 3)
        send(piece, piece, wz + z, down_z, z > 0)

    def wy_piece(d):
        return rows16(group, mod8(y - d))

    def wy_id(d):
        return recv_id(("wy", d))

    def wy_start():
        piece = wy_piece(0)
        send(piece, piece, wy_id(2), up_y2)
        send(piece, piece, wy_id(-2), down_y2)
        send(piece, piece, wy_id(1), up_y)
        send(piece, piece, wy_id(-1), down_y)
        spread(piece)

    def wy_take(d):
        piece = wy_piece(d)
        arrived(piece, wy_id(d))
        if d == 2:
            send(piece, piece, wy_id(3), up_y)
            send(piece, piece, wy_id(4), up_y2)
        if d == -2:
            send(piece, piece, wy_id(-3), down_y)
        spread(piece)

    inner = (z == 1) | (z == 2)

    def x_send(i):
        piece = rows128(order[i] * 4 + x)
        send(piece, piece, xl[i], up_x)
        send(piece, piece, xr[i], down_x)

    def z_take(i, pred=None):
        arrived(rows128(order[i] * 4 + x), wz + order[i], pred)

    def z_near():
        z_take(1)
        piece = rows128(order[1] * 4 + x)
        send(piece, piece, wz + order[1], up_z, (order[1] < z) & inner)
        x_send(1)
        z_take(2, inner)
        piece = rows128(order[2] * 4 + x)
        send(piece, piece, wz + order[2], down_z, (order[2] > z) & inner)

    def z_mid_event():
        z_take(2, (z == 0) | (z == 3))
        z_take(3, inner)
        piece = rows128(order[3] * 4 + x)
        send(piece, piece, wz + order[3], down_z, z == 1)
        send(piece, piece, wz + order[3], up_z, z == 2)
        x_send(2)

    def z_last():
        z_take(3, (z == 0) | (z == 3))
        x_send(3)

    def x_full(i):
        left = order[i] * 4 + lax.rem(x + 3, 4)
        right = order[i] * 4 + lax.rem(x + 1, 4)
        arrived(rows128(left), xl[i])
        send(rows64(left, 0), rows64(left, 0), hl[i], up_x)
        arrived(rows128(right), xr[i])
        send(rows64(right, 1), rows64(right, 1), hr[i], down_x)

    def x_half(i):
        across = order[i] * 4 + lax.rem(x + 2, 4)
        arrived(rows64(across, 0), hl[i])
        arrived(rows64(across, 1), hr[i])

    def kv_send(p, slot, to_slot, device, pred=None):
        send(kv.at[p, slot], kv.at[p, to_slot], recv_id(("kv", to_slot, p)), device, pred)

    def kv_wait(p, slot, pred=None):
        arrived(kv.at[p, slot], recv_id(("kv", slot, p)), pred)

    def kv_own(p):
        kv_send(p, 8, 7, up_y, y < 7)
        kv_send(p, 8, 0, next_line)
        kv_send(p, 8, 1, down_y, y == 0)
        kv_send(p, 8, 2, down_y2, y == 1)

    def kv_step(r, p):
        m = r - 1
        kv_wait(p, m, y <= 7 - m)
        if r == 1:
            kv_send(p, 0, 7, up_y, y == 7)
            kv_send(p, 0, 6, up_y2, y == 6)
        if r <= 4:
            kv_send(p, m, r, down_y, (y <= 7 - m) & (y > 0))
            kv_wait(p, 8 - r, y >= r)
            if r < 4:
                kv_send(p, 8 - r, 7 - r, up_y, (y >= r) & (y < 7))
            else:
                kv_send(p, 4, 3, up_y, y == 6)
        else:
            kv_send(p, 4, 5, down_y, y == 1)
            kv_wait(p, 3, y == 7)

    def kv_side(r, p):
        if r == 1:
            kv_wait(p, 1, y == 7)
            kv_send(p, 1, 2, down_y, y == 7)
            kv_wait(p, 2, y == 7)
            kv_send(p, 2, 3, down_y, y == 7)
        if r == 2:
            kv_wait(p, 2, y == 6)
            kv_send(p, 2, 3, down_y, y == 6)
            kv_wait(p, 7, y == 0)
            kv_send(p, 7, 6, up_y, y == 0)
            kv_wait(p, 6, y == 0)
            kv_send(p, 6, 5, up_y, y == 0)
        if r == 3:
            kv_wait(p, 3, y == 6)
            kv_wait(p, 3, y == 5)
            kv_wait(p, 6, y == 1)
            kv_send(p, 6, 5, up_y, y == 1)
            kv_wait(p, 5, y == 1)
        if r == 4:
            kv_wait(p, 5, y == 2)
        if r == 5:
            kv_wait(p, 5, y == 0)

    depth = lax.select(x == 3, 0, lax.select(x == 1, 2, 1)) + 3 - z
    tree_up = (z == 3) & ((x == 3) | (x == 0))
    tree_down = (z == 3) & (x == 3)
    tree_copies = []
    for p in range(2):
        piece = lkv.at[p, y]
        tree_id = recv_id(("tree", p))
        for device, pred in ((up_x, tree_up), (down_x, tree_down), (down_z, z > 0)):
            tree_copies.append((remote(piece, piece, tree_id, device), pred))
    sent.extend(tree_copies)

    def tree(k, p):
        here = depth == k
        if k:
            arrived(lkv.at[p, y], recv_id(("tree", p)), here)
        for copy, pred in tree_copies[3 * p:3 * p + 3]:
            pl.when(here & pred)(lambda copy=copy: copy.start())

    def l_up(k, p):
        last = 4 - p
        if k > last:
            return
        piece = lkv.at[p, mod8(y - k)]
        if k:
            arrived(piece, recv_id(("lp", k, p)))
        if k < last:
            send(piece, piece, recv_id(("lp", k + 1, p)), up_y)

    def l_down(k, p):
        last = 3 + p
        if k > last:
            return
        piece = lkv.at[p, lax.rem(y + k, 8)]
        if k:
            arrived(piece, recv_id(("lm", k, p)))
        if k < last:
            send(piece, piece, recv_id(("lm", k + 1, p)), down_y)

    def l_step(k):
        for p in range(2):
            l_up(k, p)
            l_down(k, p)

    def prefix_pair(i):
        keys = kv[0, :, :, i * HD:(i + 1) * HD].reshape(9 * TOK, HD)
        vals = kv[1, :, :, i * HD:(i + 1) * HD].reshape(9 * TOK, HD)
        for half in range(2):
            c = (2 * i + half) * HD
            scores = score_dot(q[:, c:c + HD], keys)
            row = lax.broadcasted_iota(jnp.int32, scores.shape, 0)
            col = lax.broadcasted_iota(jnp.int32, scores.shape, 1)
            allowed = (col > row) & (col <= row + WINDOW) & (col >= (8 - seq) * TOK)
            scores = jnp.where(allowed, scores, -jnp.inf)
            abuf[head, i, 0:TOK, half * HD:(half + 1) * HD] = softmax_dot(
                scores, vals
            ).astype(jnp.bfloat16)

    def option_pair(i):
        keys = lkv[0, :, :, i * HD:(i + 1) * HD].reshape(WINDOW, HD)
        vals = lkv[1, :, :, i * HD:(i + 1) * HD].reshape(WINDOW, HD)
        own_keys = ok[:, i * HD:(i + 1) * HD]
        own_vals = ov[:, i * HD:(i + 1) * HD]
        for half in range(2):
            c = (2 * i + half) * HD
            query = oq[:, c:c + HD]
            shared = score_dot(query, keys)
            own = score_dot(query, own_keys)
            row = lax.broadcasted_iota(jnp.int32, shared.shape, 0)
            col = lax.broadcasted_iota(jnp.int32, shared.shape, 1)
            shared = jnp.where(col > row, shared, -jnp.inf)
            row = lax.broadcasted_iota(jnp.int32, own.shape, 0)
            col = lax.broadcasted_iota(jnp.int32, own.shape, 1)
            own = jnp.where(col <= row, own, -jnp.inf)
            top = jnp.maximum(
                jnp.max(shared, axis=1, keepdims=True), jnp.max(own, axis=1, keepdims=True)
            )
            ws = jnp.exp2((shared - top) * exp2_scale)
            wo = jnp.exp2((own - top) * exp2_scale)
            total = jnp.sum(ws, axis=1, keepdims=True) + jnp.sum(wo, axis=1, keepdims=True)
            out = jnp.dot(ws.astype(jnp.bfloat16), vals, preferred_element_type=jnp.float32)
            out = out + jnp.dot(
                wo.astype(jnp.bfloat16), own_vals, preferred_element_type=jnp.float32
            )
            abuf[head, i, TOK:ROWS, half * HD:(half + 1) * HD] = (out / total).astype(
                jnp.bfloat16
            )

    def part_rows(part):
        return pl.ds(0, TOK) if part == 0 else pl.ds(TOK, OPT)

    def exchange_send(part, i):
        rows = part_rows(part)
        piece = abuf.at[head, i, rows, :]
        send(piece, relay.at[i, rows, :], recv_id(("mid", part, i)), (mid_up, mid_down)[i])
        send(piece, piece, recv_id(("sib", part, i)), sib)

    def exchange_relay(part, i):
        rows = part_rows(part)
        piece = relay.at[i, rows, :]
        arrived(piece, recv_id(("mid", part, i)))
        origin = (h_down, h_up)[i]
        send(
            piece, abuf.at[origin, i, rows, :], recv_id(("far", part, i)),
            (mid_up, mid_down)[i],
        )

    def exchange_forward(part, i):
        piece = abuf.at[h_far, i, part_rows(part), :]
        arrived(piece, recv_id(("far", part, i)))
        send(piece, piece, recv_id(("farsib", part, i)), sib)

    def exchange_sib(part):
        for i in range(2):
            arrived(abuf.at[h_sib, i, part_rows(part), :], recv_id(("sib", part, i)))

    def exchange_farsib(part):
        for i in range(2):
            arrived(abuf.at[h_farsib, i, part_rows(part), :], recv_id(("farsib", part, i)))

    def project(i):
        plane = (head, h_sib, h_far, h_farsib)[i]
        part = None
        for pair in range(2):
            rows = pl.ds(pl.multiple_of(plane * 512 + pair * 256, 256), 256)
            new = jnp.dot(
                abuf[plane, pair], wbuf[rows, :], preferred_element_type=jnp.float32
            )
            part = new if part is None else part + new
        if i == 0:
            proj[...] = part
        else:
            proj[...] += part

    wy_start()
    tree(0, 0)
    tree(0, 1)
    wy_take(2)
    wy_take(-2)
    kv_own(0)
    kv_own(1)
    wy_take(1)
    wy_take(-1)
    tree(1, 0)
    tree(1, 1)
    wy_take(3)
    wy_take(-3)
    wy_take(4)
    kv_step(1, 0)
    kv_step(1, 1)
    tree(2, 0)
    tree(2, 1)
    later[0].wait()
    res[...] = rest[...].T
    z_near()
    x_full(0)
    kv_side(1, 0)
    kv_side(1, 1)
    kv_step(2, 0)
    kv_step(2, 1)
    kv_side(2, 0)
    kv_side(2, 1)
    kv_step(3, 0)
    kv_step(3, 1)
    tree(3, 0)
    tree(3, 1)
    kv_side(3, 0)
    kv_side(3, 1)
    z_mid_event()
    x_full(1)
    tree(4, 0)
    tree(4, 1)
    kv_step(4, 0)
    kv_step(4, 1)
    kv_side(4, 0)
    kv_side(4, 1)
    tree(5, 0)
    tree(5, 1)
    l_step(0)
    kv_step(5, 0)
    kv_step(5, 1)
    kv_side(5, 0)
    kv_side(5, 1)
    for copy in later[1:5]:
        copy.wait()
    prefix_pair(0)
    exchange_send(0, 0)
    l_step(1)
    prefix_pair(1)
    exchange_send(0, 1)
    z_last()
    l_step(2)
    x_full(2)
    l_step(3)
    exchange_relay(0, 0)
    x_half(0)
    l_step(4)
    exchange_relay(0, 1)
    option_pair(0)
    exchange_send(1, 0)
    option_pair(1)
    exchange_send(1, 1)
    x_full(3)
    exchange_forward(0, 0)
    exchange_forward(0, 1)
    exchange_relay(1, 0)
    exchange_relay(1, 1)
    x_half(1)
    exchange_forward(1, 0)
    exchange_forward(1, 1)
    x_half(2)
    for copy in later[5:]:
        copy.wait()
    x_half(3)
    project(0)
    exchange_sib(0)
    exchange_sib(1)
    project(1)
    project(2)
    exchange_farsib(0)
    exchange_farsib(1)
    project(3)

    square = jnp.sum(proj[...] * proj[...], axis=1, keepdims=True)
    diag = (
        lax.broadcasted_iota(jnp.int32, (128, 128), 0)
        == lax.broadcasted_iota(jnp.int32, (128, 128), 1)
    )
    row0 = jnp.sum(jnp.where(diag, square[0:128], 0.0), axis=0, keepdims=True)
    row1 = jnp.sum(jnp.where(diag[0:64], square[128:192], 0.0), axis=0, keepdims=True)
    ssq[head] = jnp.concatenate([row0, row1, jnp.zeros((6, 128), jnp.float32)], axis=0)
    mine = ssq.at[head]
    send(mine, mine, recv_id("sq0"), far)
    send(mine, mine, recv_id("sq1"), farsib)
    send(mine, mine, recv_id("sq2"), sib)
    drain()
    arrived(ssq.at[h_sib], recv_id("sq2"))
    arrived(ssq.at[h_far], recv_id("sq0"))
    arrived(ssq.at[h_farsib], recv_id("sq1"))
    total = ssq[0] + ssq[1] + ssq[2] + ssq[3]
    col0 = jnp.sum(jnp.where(diag, total[0:1], 0.0), axis=1, keepdims=True)
    col1 = jnp.sum(jnp.where(diag[0:64], total[1:2], 0.0), axis=1, keepdims=True)
    inv0 = lax.rsqrt(col0 / D + epsilon)
    inv1 = lax.rsqrt(col1 / D + epsilon)
    scale = gain[...].reshape(1, COLS)
    pout[...] = (
        (res[...].astype(jnp.float32) + proj[0:TOK, :] * inv0 * scale).astype(jnp.bfloat16).T
    )
    full = ores[...].astype(jnp.float32) + proj[TOK:ROWS, :] * inv1 * scale
    start = bounds[0, 0]
    length = bounds[0, 1]
    pos = lax.broadcasted_iota(jnp.int32, (OPT, COLS), 0)
    inside = pos < length
    out = jnp.where(inside, full, 0.0).astype(jnp.bfloat16)
    oout[...] = out
    chosen = inside & (pos >= start)
    picked = jnp.where(chosen, out.astype(jnp.float32), 0.0)
    count = jnp.broadcast_to((length - start).astype(jnp.float32), (1, COLS))
    osum[...] = jnp.sum(picked, axis=0, keepdims=True) / count
    drain()


def fused(*args):
    bf, f32 = jnp.bfloat16, jnp.float32
    vmem = pl.BlockSpec(memory_space=pltpu.VMEM)
    return pl.pallas_call(
        kernel,
        out_shape=(
            jax.ShapeDtypeStruct((COLS, TOK), bf),
            jax.ShapeDtypeStruct((OPT, COLS), bf),
            jax.ShapeDtypeStruct((1, COLS), f32),
        ),
        in_specs=[pl.BlockSpec(memory_space=pltpu.HBM)] * 10
        + [pl.BlockSpec(memory_space=pltpu.SMEM)],
        out_specs=(vmem, vmem, vmem),
        scratch_shapes=[
            pltpu.VMEM((TOK, 512), bf),
            pltpu.VMEM((OPT, 512), bf),
            pltpu.VMEM((OPT, 256), bf),
            pltpu.VMEM((OPT, 256), bf),
            pltpu.VMEM((COLS, TOK), bf),
            pltpu.VMEM((TOK, COLS), bf),
            pltpu.VMEM((OPT, COLS), bf),
            pltpu.VMEM((COLS,), f32),
            pltpu.VMEM((2, 9, TOK, 256), bf),
            pltpu.VMEM((2, 8, TOK, 256), bf),
            pltpu.VMEM((2048, COLS), bf),
            pltpu.VMEM((4, 2, ROWS, 256), bf),
            pltpu.VMEM((2, ROWS, 256), bf),
            pltpu.VMEM((ROWS, COLS), f32),
            pltpu.VMEM((4, 8, 128), f32),
            pltpu.SemaphoreType.DMA((16,)),
            pltpu.SemaphoreType.DMA((N_SEND,)),
            pltpu.SemaphoreType.DMA((N_RECV,)),
        ],
        compiler_params=pltpu.CompilerParams(
            collective_id=0, has_side_effects=True, vmem_limit_bytes=60 * 1024 * 1024
        ),
    )(*args)


def write_kernel(a_in, b_in, c_in, a_out, b_out, c_out, a, b, c, sems):
    piece = COLS // 4
    parts = [pl.ds(i * piece, piece) for i in range(4)]
    ways = [(a_in.at[r, :], a.at[r, :], a_out.at[r, :]) for r in parts]
    ways += [(b_in, b, b_out), (c_in, c, c_out)]
    reads = [pltpu.make_async_copy(w[0], w[1], sems.at[i]) for i, w in enumerate(ways)]
    writes = [pltpu.make_async_copy(w[1], w[2], sems.at[6 + i]) for i, w in enumerate(ways)]
    for read in reads:
        read.start()
    for read, write in zip(reads, writes):
        read.wait()
        write.start()
    for write in writes:
        write.wait()


def written(*results):
    hbm = pl.BlockSpec(memory_space=pltpu.HBM)
    return pl.pallas_call(
        write_kernel,
        out_shape=tuple(jax.ShapeDtypeStruct(r.shape, r.dtype) for r in results),
        in_specs=[hbm] * 3,
        out_specs=(hbm,) * 3,
        scratch_shapes=[pltpu.VMEM(r.shape, r.dtype) for r in results]
        + [pltpu.SemaphoreType.DMA((12,))],
        compiler_params=pltpu.CompilerParams(vmem_limit_bytes=60 * 1024 * 1024),
    )(*results)


def body(
    queries, keys, values, prefix_resid, opt_queries, opt_keys, opt_values, opt_resid,
    out_weight, norm_gain, option_bounds,
):
    prefix_out, option_out, option_summary = fused(
        queries, keys, values, prefix_resid.T, opt_queries[0], opt_keys[0], opt_values[0],
        opt_resid[0], out_weight, norm_gain, option_bounds,
    )
    prefix_out, option_out, option_summary = written(prefix_out, option_out, option_summary)
    return prefix_out.T, option_out[None], option_summary[None, 0]


def solution(mesh):
    return jax.shard_map(
        body,
        mesh=mesh,
        in_specs=(
            P("seq", "head"),
            P("seq", "head"),
            P("seq", "head"),
            P("seq", "head"),
            P("seq", None, "head"),
            P("seq", None, "head"),
            P("seq", None, "head"),
            P("seq", None, "head"),
            P("seq", "head"),
            P("head"),
            P("seq", None),
        ),
        out_specs=(P("seq", "head"), P("seq", None, "head"), P("seq", "head")),
        check_vma=False,
    )
```
